32 devices in a mesh: row: 4 (over y, x), col: 8 (over z, core).
Axes of the slice: x: 2, y: 2, z: 4, core: 2. Of those that a mesh axis runs over, the one named last changes fastest.
Arguments:
- node_features: bfloat16 [4096, 1024], P(('row', 'col')), may hold values from -6 to 6
- norm_gain: float32 [1024], replicated, may hold values from 0.5 to 1.5
- w_query: bfloat16 [1024, 1024], replicated, may hold values from -0.1875 to 0.1875
- w_keyvalue: bfloat16 [1024, 2048], replicated, may hold values from -0.1875 to 0.1875
- w_out: bfloat16 [1024, 1024], replicated, may hold values from -0.1875 to 0.1875
- bias_table: float32 [32, 8], replicated, may hold values from -4 to 4
- edge_slope: float32 [8], replicated, may hold values from 0.5 to 1.5
- pair_blocks: int32 [4, 8, 2, 16], P('row', 'col'), may hold values from -1 to 7, as said below
- bucket_ids: int32 [4, 8, 16, 128, 128], P('row', 'col'), may hold values from 0 to 31
- edge_weight: bfloat16 [4, 8, 4, 4, 128, 128], P('row', 'col'), may hold values from -4 to 240
Outputs:
- node_out: bfloat16 [4096, 1024], P(('row', 'col'))
The draws below stay inside these ranges and needn't reach their ends.
Inputs may be any that keep to these rules, and one draw needn't show every extreme that they name: `pair_blocks`: slots of a tile with query block -1 are empty and name key block 0. The listed pairs of a tile are distinct; each tile (r, c) lists, among the slots from t = r, every block of node shard r * 8 + c paired with itself. Up to 4 slots from one owner to one row range are used, and some tile uses all 16 of its slots.
All inputs are finite; a program needn't handle non-finite values.
Results may differ from the reference program's by a relative error of at most 0.005.
Values may be sent and summed in bfloat16 or wider, within the bound.
A program may use at most 256 MiB of HBM per device.

```python
import math
import jax
import jax.numpy as jnp
from jax import lax

D = 1024
H = 8
BLK = 128
NB = 32
NODES_DEV = 128
KB_DEV = 1
QB_ROW = 8
CAP = 4
SLOTS = 16
NODES = 4096
N_ROW = 4
N_COL = 8


def draw_edge_weight(key, part):
    full_shape = (N_ROW, N_COL, N_ROW, CAP, BLK, BLK)
    return jnp.clip(jax.random.normal(jax.random.fold_in(key, 6), full_shape, jnp.float32), -4.0, 4.0).astype(jnp.bfloat16)


def draw_pair_blocks(key, part):
    cand_count = QB_ROW * KB_DEV
    group_shape = (N_ROW, N_COL, N_ROW)
    cand_index = jnp.arange(cand_count, dtype=jnp.int32)
    rand_score = jax.random.randint(jax.random.fold_in(key, 11), group_shape + (cand_count,), 0, 1 << 16)
    order_key = rand_score * cand_count + cand_index
    dest_row = jnp.arange(N_ROW, dtype=jnp.int32).reshape(N_ROW, 1, 1, 1)
    col_index = jnp.arange(N_COL, dtype=jnp.int32).reshape(1, N_COL, 1, 1)
    source_row = jnp.arange(N_ROW, dtype=jnp.int32).reshape(1, 1, N_ROW, 1)
    query_part = cand_index // KB_DEV
    key_part = cand_index % KB_DEV
    diagonal = (dest_row == source_row) & (query_part == col_index * KB_DEV + key_part)
    order_key = jnp.where(diagonal, cand_index - cand_count, order_key)
    picked = jnp.argsort(order_key, axis=-1)[..., :CAP].astype(jnp.int32)
    live_count = jax.random.randint(jax.random.fold_in(key, 12), group_shape, 1, CAP + 1)
    full_row = jax.random.randint(jax.random.fold_in(key, 13), (), 0, N_ROW)
    full_col = jax.random.randint(jax.random.fold_in(key, 14), (), 0, N_COL)
    dest_grid = dest_row[..., 0]
    col_grid = col_index[..., 0]
    source_grid = source_row[..., 0]
    live_count = jnp.where((dest_grid == full_row) & (col_grid == full_col), CAP, live_count)
    live_count = jnp.where(dest_grid == source_grid, jnp.maximum(live_count, KB_DEV), live_count)
    slot_index = jnp.arange(CAP, dtype=jnp.int32)
    slot_live = slot_index < live_count[..., None]
    query_block = jnp.where(slot_live, picked // KB_DEV, -1)
    key_block = jnp.where(slot_live, picked % KB_DEV, 0)
    stacked = jnp.stack([query_block, key_block], axis=2)
    return stacked.reshape(N_ROW, N_COL, 2, N_ROW * CAP).astype(jnp.int32)


def set_ends(array, key, smallest, largest):
    longest = array.shape.index(max(array.shape))
    spots = []
    for shift in (0, 1):
        where = [jax.random.randint(jax.random.fold_in(key, axis), (), 0, length) for axis, length in enumerate(array.shape)]
        where[longest] = (where[longest] + shift) % array.shape[longest]
        spots.append(tuple(where))
    return array.at[spots[0]].set(smallest).at[spots[1]].set(largest)


def steps_of(rng, dims, pieces, smallest, top_value):
    level = 1.0
    for dim, parts in pieces:
        heights = jax.random.uniform(jax.random.fold_in(jax.random.fold_in(rng, 6), dim), (parts,), jnp.float32, smallest / len(pieces), top_value / len(pieces))
        level = level * jnp.repeat(jnp.exp(heights), dims[dim] // parts).reshape((-1,) + (1,) * (len(dims) - 1 - dim))
    return level


def gaussian(key, extent, width, bound, cuts=(), kind=jnp.bfloat16):
    drawn = width * jax.random.normal(key, extent, jnp.float32)
    if cuts:
        drawn = drawn * steps_of(key, extent, cuts, -0.22, 0.18)
    return jnp.clip(drawn, -bound, bound).astype(kind)


def setup_inputs(seed: int = 0) -> dict:
    key_of = jax.random.split(jax.random.key(seed), 11)
    node_features = gaussian(key_of[0], (NODES, D), 1.0, 6.0, ((0, 32),))
    norm_gain = jnp.clip(1.0 + 0.1 * jax.random.normal(key_of[1], (D,), jnp.float32), 0.5, 1.5)
    w_query = gaussian(key_of[2], (D, D), D ** -0.5, 0.1875)
    w_keyvalue = gaussian(key_of[3], (D, 2 * D), D ** -0.5, 0.1875)
    w_out = gaussian(key_of[4], (D, D), D ** -0.5, 0.1875)
    bias_table = gaussian(key_of[5], (NB, H), 1.0, 4.0, (), jnp.float32)
    edge_slope = jnp.clip(jnp.exp(jax.random.uniform(key_of[6], (H,), jnp.float32, math.log(0.5), math.log(1.5))), 0.5, 1.5)
    pair_blocks = draw_pair_blocks(jax.random.fold_in(key_of[10], 71), 0)
    bucket_ids = set_ends(jax.random.randint(key_of[8], (N_ROW, N_COL, SLOTS, BLK, BLK), 0, NB), jax.random.fold_in(key_of[8], 1), 0, NB - 1).astype(jnp.int32)
    edge_weight = draw_edge_weight(jax.random.fold_in(key_of[10], 71), 0)
    return {"node_features": node_features, "norm_gain": norm_gain, "w_query": w_query, "w_keyvalue": w_keyvalue, "w_out": w_out, "bias_table": bias_table, "edge_slope": edge_slope, "pair_blocks": pair_blocks, "bucket_ids": bucket_ids, "edge_weight": edge_weight}


EPSILON = 1e-05
LOW_FLOOR = -1e+30

def normalize(features, gain_vec):
    as_float = features.astype(jnp.float32)
    centered = as_float - lax.optimization_barrier(jnp.mean(as_float, axis=-1, keepdims=True))
    variance = lax.optimization_barrier(jnp.mean(centered * centered, axis=-1, keepdims=True))
    return (centered * lax.rsqrt(variance + EPSILON) * gain_vec).astype(jnp.bfloat16)

def slot_terms(query_range, key_group, value_group, query_block, key_block, tile_weights, tile_buckets, bias_table, edge_slope):
    head_count = edge_slope.shape[0]
    head_dim = query_range.shape[1] // head_count
    query_start = (jnp.maximum(query_block, 0) * BLK).astype(jnp.int32)
    key_start = (key_block * BLK).astype(jnp.int32)
    query_tile = lax.dynamic_slice_in_dim(query_range, query_start, BLK, 0).astype(jnp.float32).reshape(BLK, head_count, head_dim)
    key_tile = lax.dynamic_slice_in_dim(key_group, key_start, BLK, 0).astype(jnp.float32).reshape(BLK, head_count, head_dim)
    value_tile = lax.dynamic_slice_in_dim(value_group, key_start, BLK, 0).astype(jnp.float32).reshape(BLK, head_count, head_dim)
    raw_score = jnp.einsum('ihd,jhd->hij', query_tile, key_tile) * head_dim ** (-0.5)
    raw_score = raw_score + jnp.transpose(bias_table[tile_buckets], (2, 0, 1))
    raw_score = raw_score + edge_slope[:, None, None] * tile_weights.astype(jnp.float32)[None]
    row_max = lax.optimization_barrier(jnp.max(raw_score, axis=-1))
    rounded = lax.optimization_barrier(jnp.exp(raw_score - row_max[:, :, None]).astype(jnp.bfloat16))
    prob_vals = rounded.astype(jnp.float32)
    row_sum = lax.optimization_barrier(jnp.sum(prob_vals, axis=-1))
    weighted = jnp.einsum('hij,jhd->ihd', prob_vals, value_tile)
    return (row_max, row_sum, weighted)

def tile_partials(query_range, key_group, value_group, pair_table, edge_values, bucket_tiles, bias_table, edge_slope):
    range_rows = query_range.shape[0]
    head_count = edge_slope.shape[0]
    head_dim = query_range.shape[1] // head_count
    slot_count = pair_table.shape[1]
    slot_cap = slot_count // N_ROW
    key_blocks = NODES_DEV // BLK
    initial = (jnp.full((range_rows, head_count), LOW_FLOOR, jnp.float32), jnp.zeros((range_rows, head_count), jnp.float32), jnp.zeros((range_rows, head_count, head_dim), jnp.float32))

    def advance(carry, inputs):
        max_all, sum_all, out_all = carry
        query_block, key_part, tile_weights, tile_buckets, slot_index = inputs
        key_block = key_part + slot_index // slot_cap * key_blocks
        row_max, row_sum, weighted = slot_terms(query_range, key_group, value_group, query_block, key_block, tile_weights, tile_buckets, bias_table, edge_slope)
        row_start = (jnp.maximum(query_block, 0) * BLK).astype(jnp.int32)
        old_max = lax.dynamic_slice_in_dim(max_all, row_start, BLK, 0)
        old_sum = lax.dynamic_slice_in_dim(sum_all, row_start, BLK, 0)
        old_out = lax.dynamic_slice_in_dim(out_all, row_start, BLK, 0)
        new_max = jnp.maximum(old_max, row_max.T)
        left_scale = jnp.exp(old_max - new_max)
        right_scale = jnp.exp(row_max.T - new_max)
        new_sum = old_sum * left_scale + row_sum.T * right_scale
        new_out = old_out * left_scale[:, :, None] + weighted * right_scale[:, :, None]
        slot_live = query_block >= 0
        new_max = jnp.where(slot_live, new_max, old_max)
        new_sum = jnp.where(slot_live, new_sum, old_sum)
        new_out = jnp.where(slot_live, new_out, old_out)
        max_all = lax.dynamic_update_slice_in_dim(max_all, new_max, row_start, 0)
        sum_all = lax.dynamic_update_slice_in_dim(sum_all, new_sum, row_start, 0)
        out_all = lax.dynamic_update_slice_in_dim(out_all, new_out, row_start, 0)
        return ((max_all, sum_all, out_all), None)
    carry, _ = lax.scan(advance, initial, (pair_table[0], pair_table[1], edge_values, bucket_tiles, jnp.arange(slot_count, dtype=jnp.int32)))
    return carry

def reference(node_features, norm_gain, w_query, w_keyvalue, w_out, bias_table, edge_slope, pair_blocks, bucket_ids, edge_weight):
    model_width = node_features.shape[1]
    head_count = edge_slope.shape[0]
    head_dim = model_width // head_count
    normalized = normalize(node_features, norm_gain)
    queries = jnp.dot(normalized, w_query, preferred_element_type=jnp.float32).astype(jnp.bfloat16)
    key_value = jnp.dot(normalized, w_keyvalue, preferred_element_type=jnp.float32).astype(jnp.bfloat16)
    range_rows = N_COL * NODES_DEV
    query_rows = queries.reshape(N_ROW, range_rows, model_width)
    grouped = key_value.reshape(N_ROW, N_COL, NODES_DEV, 2 * model_width)
    slot_count = N_ROW * CAP

    def row_range(row_index):
        query_range = query_rows[row_index]

        def one_col(carry, col_index):
            key_group = grouped[:, col_index].reshape(N_ROW * NODES_DEV, 2 * model_width)
            edge_values = edge_weight[:, col_index, row_index].reshape(slot_count, BLK, BLK)
            col_max, col_sum, col_out = tile_partials(query_range, key_group[:, :model_width], key_group[:, model_width:], pair_blocks[row_index, col_index], edge_values, bucket_ids[row_index, col_index], bias_table, edge_slope)
            max_all, sum_all, out_all = carry
            new_max = jnp.maximum(max_all, col_max)
            left_scale = jnp.exp(max_all - new_max)
            right_scale = jnp.exp(col_max - new_max)
            return ((new_max, sum_all * left_scale + col_sum * right_scale, out_all * left_scale[:, :, None] + col_out * right_scale[:, :, None]), None)
        initial = (jnp.full((range_rows, head_count), LOW_FLOOR, jnp.float32), jnp.zeros((range_rows, head_count), jnp.float32), jnp.zeros((range_rows, head_count, head_dim), jnp.float32))
        (max_all, sum_all, out_all), _ = lax.scan(one_col, initial, jnp.arange(N_COL, dtype=jnp.int32))
        return (out_all / sum_all[:, :, None]).astype(jnp.bfloat16).reshape(range_rows, model_width)
    attention = lax.map(row_range, jnp.arange(N_ROW, dtype=jnp.int32)).reshape(N_ROW * range_rows, model_width)
    update = jnp.dot(attention, w_out, preferred_element_type=jnp.float32)
    return (node_features.astype(jnp.float32) + update).astype(jnp.bfloat16)
```

```python
import functools

import jax
import jax.numpy as jnp
from jax import lax
from jax.experimental import pallas as pl
from jax.experimental.pallas import tpu as pltpu
from jax.sharding import PartitionSpec as P

EPSILON = 1e-05
LOW_FLOOR = -1e30
CORES = 2
MESH = pl.DeviceIdType.MESH
LANES = 128
CHUNK_HEADS = 2
TAIL = 16
EARLY_BYTES = 12 * 2**20
VMEM_BYTES = 67043328


def normalize(features, gain_vec):
    as_float = features.astype(jnp.float32)
    centered = as_float - jnp.mean(as_float, axis=-1, keepdims=True)
    variance = jnp.mean(centered * centered, axis=-1, keepdims=True)
    return (centered * lax.rsqrt(variance + EPSILON) * gain_vec).astype(jnp.bfloat16)


def target_of(index, k, n):
    if n & (n - 1):
        return (index + k) % n
    return index ^ k


def source_of(index, k, n):
    if n & (n - 1):
        return (index + n - k) % n
    return index ^ k


def pick(index, values):
    if all(v == values[0] for v in values):
        return values[0]
    out = values[0]
    for at, value in enumerate(values[1:], 1):
        out = jnp.where(index == at, value, out)
    return out


def proxied(source, dest, n):
    return (source == 0 and dest >= 2) or (source == n - 1 and dest <= n - 3)


def route_tables(n):
    now, later, incoming = [], [], []
    for z in range(n):
        others = sorted((d for d in range(n) if d != z), key=lambda d: -abs(d - z))
        relay = {d for d in others if (z == 1 and proxied(0, d, n)) or (z == n - 2 and proxied(n - 1, d, n))}
        now.append([d for d in others if d not in relay])
        later.append([d for d in others if d in relay])
        incoming.append([s for s in others[::-1] if not proxied(s, z, n)])
    return now, later, incoming


def padded(rows, fill):
    longest = max(map(len, rows))
    return [[row[j] if j < len(row) else fill(z) for z, row in enumerate(rows)] for j in range(longest)]


def split_level(level):
    high = level.astype(jnp.bfloat16).astype(jnp.float32)
    rest = level - high
    middle = rest.astype(jnp.bfloat16).astype(jnp.float32)
    low = rest - middle
    filler = jnp.zeros((TAIL - 3 * level.shape[0], level.shape[1]), jnp.float32)
    return jnp.concatenate([high, middle, low, filler], axis=0).astype(jnp.bfloat16)


def join_level(tail, count):
    tail = tail.astype(jnp.float32)
    return tail[:count] + tail[count : 2 * count] + tail[2 * count : 3 * count]


def layer(
    n_row, n_chip, early, scale, pairs, slope, x_in, gain_in, wq_in, wkv_in, wo_in, table_in, b_in, e_in, out_ref, *scratch
):
    scratch = list(scratch)
    chunks = x_in.shape[1] // (CHUNK_HEADS * (x_in.shape[1] // slope.shape[0]))
    q_all = [scratch.pop(0) for _ in range(chunks)]
    (
        x_buf, n_in, n_buf, wq_buf, wkv_buf, wo_buf, k_buf, v_buf, b_buf, e_all, bias, table,
        o_slot, m_slot, s_slot, codes, lookup, sib_out, sib_in, mix_out, via_in, got_in, own_o, own_l, acc,
        load_sem, x_sem, e_sem, q_send, q_recv, pair_send, pair_recv,
        sib_send, sib_recv, mix_send, via_recv, got_recv,
    ) = scratch
    row, col = lax.axis_index("row"), lax.axis_index("col")
    chip, core = col // CORES, col % CORES
    n_col = n_chip * CORES
    tile, width = x_in.shape
    heads = slope.shape[0]
    dim = width // heads
    hc = CHUNK_HEADS
    cw = hc * dim
    slot_cap = e_in.shape[1]
    slots = n_row * slot_cap
    f32, bf16 = jnp.float32, jnp.bfloat16
    sibling = (row, chip * CORES + (1 - core))
    chip_at = lambda z: (row, z * CORES + core)
    targets = [target_of(row, k, n_row) for k in range(1, n_row)]
    sources = [source_of(row, k, n_row) for k in range(1, n_row)]

    def load(src, dst, spot):
        copy = pltpu.make_async_copy(src, dst, load_sem.at[spot])
        copy.start()
        return copy

    def remote(src, dst, send, recv, where):
        return pltpu.make_async_remote_copy(
            src_ref=src, dst_ref=dst, send_sem=send, recv_sem=recv, device_id=where, device_id_type=MESH
        )

    x_load = load(x_in, x_buf, 0)
    wq_load = load(wq_in, wq_buf, 1)
    barrier = pltpu.get_barrier_semaphore()
    partners = [chip_at(target_of(chip, k, n_chip)) for k in range(1, n_chip)]
    if n_chip & (n_chip - 1):
        partners = [chip_at((chip + k) % n_chip) for k in range(1, n_chip)]
    partners = partners + [sibling] + [(r, col) for r in targets]
    for where in partners:
        pl.semaphore_signal(barrier, inc=1, device_id=where, device_id_type=MESH)
    b_load = load(b_in, b_buf, 2)
    own_e = load(e_in.at[row], e_all.at[row], 3)
    wkv_load = load(wkv_in, wkv_buf, 4)
    wo_load = load(wo_in, wo_buf, 5)

    table[...] = jnp.zeros(table.shape, f32)
    table[:, : table_in.shape[1]] = table_in[...]
    o_slot[slots] = jnp.zeros(o_slot.shape[1:], f32)
    m_slot[slots] = jnp.full(m_slot.shape[1:], LOW_FLOOR, f32)
    s_slot[slots] = jnp.zeros(s_slot.shape[1:], f32)

    x_load.wait()
    n_in[...] = normalize(x_buf[...], gain_in[...])
    pl.semaphore_wait(barrier, len(partners))

    x_copies = [
        remote(n_in, n_buf.at[k], x_sem.at[0, k], x_sem.at[1, k], (targets[k], col)) for k in range(n_row - 1)
    ]
    e_copies = [
        remote(e_in.at[targets[k]], e_all.at[row], e_sem.at[0, k], e_sem.at[1, k], (targets[k], col))
        for k in range(n_row - 1)
    ]
    for copy in x_copies + e_copies:
        copy.start()

    def e_arrival(k):
        there = e_all.at[sources[k]]
        return remote(there, there, e_sem.at[0, k], e_sem.at[1, k], (targets[k], col))

    def q_copy(c, k):
        here = q_all[c].at[col]
        return remote(here, here, q_send.at[c, k], q_recv.at[c, k], chip_at(target_of(chip, k + 1, n_chip)))

    def q_arrival(c, k):
        there = q_all[c].at[source_of(chip, k + 1, n_chip) * CORES + core]
        return remote(there, there, q_send.at[c, k], q_recv.at[c, k], sibling)

    def pair_copy(c, k, mine):
        origin = source_of(chip, k, n_chip) if k else chip
        there = q_all[c].at[origin * CORES + (core if mine else 1 - core)]
        return remote(there, there, pair_send.at[c, k], pair_recv.at[c, k], sibling)

    wq_load.wait()
    for c in range(chunks):
        cols = slice(c * cw, (c + 1) * cw)
        q_all[c][col] = jnp.dot(n_in[...], wq_buf[:, cols], preferred_element_type=f32).astype(bf16)
        for k in reversed(range(n_chip - 1)):
            q_copy(c, k).start()
        pair_copy(c, 0, True).start()

    @pl.loop(0, slots)
    def _(v):
        codes[v] = jnp.where(pairs[0, v] >= 0, pairs[0, v] * n_row + pairs[1, v] + v // slot_cap, -1)

    @pl.loop(0, n_col * n_row)
    def _(spot):
        found = jnp.int32(slots)
        for v in range(slots):
            found = jnp.where(codes[v] == spot, v, found)
        lookup[spot] = found

    def make_bias(owner, first, count):
        def one(k, carry):
            slot = owner * slot_cap + k
            buckets = b_buf[slot].T
            edges = e_all[owner, k].astype(f32).T
            for j in range(count):
                h = first + j
                entries = jnp.broadcast_to(table[h : h + 1, :], (tile, tile))
                picked = jnp.take_along_axis(entries, buckets, axis=1, mode="promise_in_bounds")
                bias[slot, j] = picked + slope[h] * edges
            return carry

        lax.fori_loop(0, slot_cap, one, 0)

    step = min(2 * LANES, width)

    def project(rows_ref, spot):
        hidden = rows_ref[...]

        @pl.loop(0, width // step)
        def _(at):
            left = pl.multiple_of(at * step, step)
            k_buf[spot, :, pl.ds(left, step)] = jnp.dot(
                hidden, wkv_buf[:, pl.ds(left, step)], preferred_element_type=f32
            ).astype(bf16)
            right = pl.multiple_of(width + left, step)
            value = jnp.dot(hidden, wkv_buf[:, pl.ds(right, step)], preferred_element_type=f32)
            v_buf[spot, pl.ds(left, step), :] = value.T.astype(bf16)

    def forward(c):
        for k in range(n_chip - 1):
            q_arrival(c, k).wait_recv()
            pair_copy(c, k + 1, True).start()

    b_load.wait()
    own_e.wait()
    if early:
        make_bias(row, 0, heads)
    wkv_load.wait()
    project(n_in, row)
    for k in range(n_row - 1):
        x_copies[k].wait_recv()
        project(n_buf.at[k], sources[k])
    forward(0)
    for k in range(n_row - 1):
        e_arrival(k).wait_recv()
        if early:
            make_bias(sources[k], 0, heads)

    group = slot_cap

    def attend(c):
        if not early:
            for r in range(n_row):
                make_bias(r, c * hc, hc)

        def one(t, carry):
            for k in range(group):
                v = t * group + k
                query = jnp.maximum(pairs[0, v], 0)
                key = pairs[1, v] + v // slot_cap
                tops, sums = [], []
                for j in range(hc):
                    h = c * hc + j
                    score = lax.dot_general(
                        k_buf[key, :, h * dim : (h + 1) * dim],
                        q_all[c][query, :, j * dim : (j + 1) * dim],
                        (((1,), (1,)), ((), ())),
                        preferred_element_type=f32,
                    )
                    score = score * scale + bias[v, h if early else j]
                    top = jnp.max(score, axis=0, keepdims=True)
                    probs = jnp.exp(score - top).astype(bf16)
                    tops.append(top)
                    sums.append(jnp.sum(probs.astype(f32), axis=0, keepdims=True))
                    o_slot[v, j * dim : (j + 1) * dim, :] = jnp.dot(
                        v_buf[key, h * dim : (h + 1) * dim, :], probs, preferred_element_type=f32
                    )
                m_slot[v] = jnp.concatenate(tops, axis=0)
                s_slot[v] = jnp.concatenate(sums, axis=0)
            return carry

        lax.fori_loop(0, slots // group, one, 0)

    def combine(levels, weights_of, parts):
        top = functools.reduce(jnp.maximum, levels)
        shares = [jnp.exp(level - top) for level in levels]
        total = functools.reduce(jnp.add, [s if w is None else s * w for s, w in zip(shares, weights_of)])
        live = total > 0.0
        safe = jnp.where(live, total, 1.0)
        level = jnp.where(live, top + jnp.log(safe), LOW_FLOOR)
        inverse = 1.0 / safe
        shares = [share * inverse for share in shares]
        out = []
        for j in range(hc):
            rows = slice(j * dim, (j + 1) * dim)
            out.append(
                functools.reduce(jnp.add, [s[j : j + 1] * part(rows).astype(f32) for s, part in zip(shares, parts)])
            )
        return out, level

    def reader(ref):
        return lambda rows: ref[rows, :]

    def merge(block, extras):
        levels, weights, parts = [], [], []
        for r in range(n_row):
            v = lookup[block * n_row + r]
            levels.append(m_slot[v])
            weights.append(s_slot[v])
            parts.append(functools.partial(lambda v, rows: o_slot[v, rows, :], v))
        for ref in extras:
            levels.append(join_level(ref[cw : cw + TAIL, :], hc))
            weights.append(None)
            parts.append(reader(ref))
        return combine(levels, weights, parts)

    def put(ref, out, level):
        for j in range(hc):
            ref[j * dim : (j + 1) * dim, :] = out[j].astype(bf16)
        ref[cw : cw + TAIL, :] = split_level(level)

    now, later, incoming = route_tables(n_chip)
    now_at = padded(now, lambda z: z)
    later_at = padded(later, lambda z: z) if any(later) else []
    from_at = padded(incoming, lambda z: z)

    def sib_copy(c, z, mine):
        return remote(sib_out.at[c, z], sib_in.at[c, z], sib_send.at[c, z], sib_recv.at[c, z], sibling)

    def far_order():
        return [pick(chip, [sorted(range(n_chip), key=lambda d: -abs(d - z))[j] for z in range(n_chip)]) for j in range(n_chip)]

    order = far_order()

    def to_sibling(c):
        for z in order:
            put(sib_out.at[c, z], *merge(z * CORES + (1 - core), []))
            sib_copy(c, z, True).start()

    def direct(c, z):
        return remote(mix_out.at[c, z], got_in.at[c, chip], mix_send.at[c, z], got_recv.at[c, chip], chip_at(z))

    def got_from(c, s):
        return remote(mix_out.at[c, s], got_in.at[c, s], mix_send.at[c, s], got_recv.at[c, s], chip_at(s))

    def to_proxy(c, z):
        where = pick(chip, [1 if at == 0 else n_chip - 2 for at in range(n_chip)])
        return remote(mix_out.at[c, z], via_in.at[c, z], mix_send.at[c, z], via_recv.at[c, z], chip_at(where))

    def flags(rows):
        return [[1 if j < len(row) else 0 for row in rows] for j in range(max(map(len, rows)))]

    now_flags, later_flags, from_flags = flags(now), flags(later), flags(incoming)

    def guard(values, run):
        if all(values):
            run()
        elif any(values):
            pl.when(pick(chip, values) == 1)(run)

    def send_now(c):
        for j, dests in enumerate(now_at):
            z = pick(chip, dests)
            passes = [int(f and proxied(at, d, n_chip)) for at, (f, d) in enumerate(zip(now_flags[j], dests))]
            straight = [int(f and not proxied(at, d, n_chip)) for at, (f, d) in enumerate(zip(now_flags[j], dests))]

            def run(z=z, passes=passes, straight=straight):
                sib_copy(c, z, False).wait_recv()
                put(mix_out.at[c, z], *merge(z * CORES + core, [sib_in.at[c, z]]))
                guard(passes, lambda: to_proxy(c, z).start())
                guard(straight, lambda: direct(c, z).start())

            guard(now_flags[j], run)
        sib_copy(c, chip, False).wait_recv()
        out, level = merge(chip * CORES + core, [sib_in.at[c, chip]])
        for j in range(hc):
            own_o[c, j * dim : (j + 1) * dim, :] = out[j]
        own_l[c] = level

    def send_later(c):
        for j, dests in enumerate(later_at):
            z = pick(chip, dests)

            def run(z=z):
                sib_copy(c, z, False).wait_recv()
                to_proxy(c, z).wait_recv()
                put(mix_out.at[c, z], *merge(z * CORES + core, [sib_in.at[c, z], via_in.at[c, z]]))
                direct(c, z).start()

            guard(later_flags[j], run)

    for j, origins in enumerate(from_at):
        if not all(from_flags[j]):
            s = pick(chip, origins)

            def blank(s=s):
                for c in range(chunks):
                    got_in[c, s, :cw, :] = jnp.zeros((cw, tile), bf16)
                    got_in[c, s, cw:, :] = split_level(jnp.full((hc, tile), LOW_FLOOR, f32))

            guard([1 - f for f in from_flags[j]], blank)

    def finish(c):
        levels, parts = [own_l[c]], [lambda rows: own_o[c, rows, :]]
        for j, origins in enumerate(from_at):
            s = pick(chip, origins)
            guard(from_flags[j], lambda: got_from(c, s).wait_recv())
            ref = got_in.at[c, s]
            levels.append(join_level(ref[cw : cw + TAIL, :], hc))
            parts.append(reader(ref))
        out, _ = combine(levels, [None] * len(levels), parts)
        attention = jnp.concatenate([o.astype(bf16) for o in out], axis=0)
        update = lax.dot_general(
            attention, wo_buf[c * cw : (c + 1) * cw, :], (((0,), (0,)), ((), ())), preferred_element_type=f32
        )
        if c == 0:
            acc[...] = x_buf[...].astype(f32) + update
        elif c < chunks - 1:
            acc[...] += update
        else:
            out_ref[...] = (acc[...] + update).astype(out_ref.dtype)

    wo_load.wait()
    for c in range(chunks):
        for k in range(n_chip):
            pair_copy(c, k, False).wait_recv()
        if c + 1 < chunks:
            forward(c + 1)
        attend(c)
        to_sibling(c)
        send_now(c)
        send_later(c)
        if c:
            finish(c - 1)
    finish(chunks - 1)

    for copy in x_copies + e_copies:
        copy.wait_send()
    for c in range(chunks):
        for k in range(n_chip - 1):
            q_copy(c, k).wait_send()
        for k in range(n_chip):
            pair_copy(c, k, True).wait_send()
            sib_copy(c, k, True).wait_send()
        for k in range(n_chip - 1):
            z = target_of(chip, k + 1, n_chip)
            direct(c, z).wait_send()


def local(
    n_row,
    n_col,
    node_features,
    norm_gain,
    w_query,
    w_keyvalue,
    w_out,
    bias_table,
    edge_slope,
    pair_blocks,
    bucket_ids,
    edge_weight,
):
    tile, width = node_features.shape
    heads = edge_slope.shape[0]
    dim = width // heads
    n_chip = n_col // CORES
    slot_cap = edge_weight.shape[3]
    slots = n_row * slot_cap
    hc = CHUNK_HEADS
    cw = hc * dim
    chunks = heads // hc
    bf16, f32 = jnp.bfloat16, jnp.float32
    vmem = pl.BlockSpec(memory_space=pltpu.VMEM)
    smem = pl.BlockSpec(memory_space=pltpu.SMEM)
    hbm = pl.BlockSpec(memory_space=pl.ANY)
    early = 4 * slots * heads * tile * tile <= EARLY_BYTES
    message = (chunks, n_chip, cw + TAIL, tile)
    dma = pltpu.SemaphoreType.DMA
    scratch = [pltpu.VMEM((n_col, tile, cw), bf16)] * chunks + [
        pltpu.VMEM((tile, width), bf16),
        pltpu.VMEM((tile, width), bf16),
        pltpu.VMEM((n_row - 1, tile, width), bf16),
        pltpu.VMEM(w_query.shape, bf16),
        pltpu.VMEM(w_keyvalue.shape, bf16),
        pltpu.VMEM(w_out.shape, bf16),
        pltpu.VMEM((n_row, tile, width), bf16),
        pltpu.VMEM((n_row, width, tile), bf16),
        pltpu.VMEM((slots, tile, tile), jnp.int32),
        pltpu.VMEM((n_row,) + edge_weight.shape[3:], bf16),
        pltpu.VMEM((slots, heads if early else hc, tile, tile), f32),
        pltpu.VMEM((heads, tile), f32),
        pltpu.VMEM((slots + 1, cw, tile), f32),
        pltpu.VMEM((slots + 1, hc, tile), f32),
        pltpu.VMEM((slots + 1, hc, tile), f32),
        pltpu.SMEM((slots,), jnp.int32),
        pltpu.SMEM((n_col * n_row,), jnp.int32),
        pltpu.VMEM(message, bf16),
        pltpu.VMEM(message, bf16),
        pltpu.VMEM(message, bf16),
        pltpu.VMEM(message, bf16),
        pltpu.VMEM(message, bf16),
        pltpu.VMEM((chunks, cw, tile), f32),
        pltpu.VMEM((chunks, hc, tile), f32),
        pltpu.VMEM((tile, width), f32),
        dma((6,)),
        dma((2, n_row - 1)),
        dma((2, n_row - 1)),
        dma((chunks, n_chip - 1)),
        dma((chunks, n_chip - 1)),
        dma((chunks, n_chip)),
        dma((chunks, n_chip)),
        dma((chunks, n_chip)),
        dma((chunks, n_chip)),
        dma((chunks, n_chip)),
        dma((chunks, n_chip)),
        dma((chunks, n_chip)),
    ]
    return pl.pallas_call(
        functools.partial(layer, n_row, n_chip, early, dim ** (-0.5)),
        out_shape=jax.ShapeDtypeStruct((tile, width), bf16),
        in_specs=[smem, smem, hbm, vmem, hbm, hbm, hbm, vmem, hbm, hbm],
        out_specs=vmem,
        scratch_shapes=scratch,
        compiler_params=pltpu.CompilerParams(collective_id=0, has_side_effects=True, vmem_limit_bytes=VMEM_BYTES),
        name="layer",
    )(
        pair_blocks.reshape(2, slots),
        edge_slope,
        node_features,
        norm_gain[None],
        w_query,
        w_keyvalue,
        w_out,
        bias_table.T,
        bucket_ids.reshape(slots, tile, tile),
        edge_weight[0, 0],
    )


def solution(mesh):
    return jax.shard_map(
        functools.partial(local, mesh.shape["row"], mesh.shape["col"]),
        mesh=mesh,
        in_specs=(
            P(("row", "col"), None),
            P(),
            P(),
            P(),
            P(),
            P(),
            P(),
            P("row", "col", None, None),
            P("row", "col", None, None, None),
            P("row", "col", None, None, None, None),
        ),
        out_specs=P(("row", "col"), None),
        check_vma=False,
    )
```

```python
import functools

import jax
import jax.numpy as jnp
from jax import lax
from jax.experimental import pallas as pl
from jax.experimental.pallas import tpu as pltpu
from jax.sharding import PartitionSpec as P

EPSILON = 1e-05
LOW_FLOOR = -1e30
CORES = 2
MESH = pl.DeviceIdType.MESH
LANES = 128
CHUNK_HEADS = 2
TAIL = 16
EARLY_BYTES = 12 * 2**20
VMEM_BYTES = 67043328


def normalize(features, gain_vec):
    as_float = features.astype(jnp.float32)
    centered = as_float - jnp.mean(as_float, axis=-1, keepdims=True)
    variance = jnp.mean(centered * centered, axis=-1, keepdims=True)
    return (centered * lax.rsqrt(variance + EPSILON) * gain_vec).astype(jnp.bfloat16)


def target_of(index, k, n):
    if n & (n - 1):
        return (index + k) % n
    return index ^ k


def source_of(index, k, n):
    if n & (n - 1):
        return (index + n - k) % n
    return index ^ k


def pick(index, values):
    if all(v == values[0] for v in values):
        return values[0]
    out = values[0]
    for at, value in enumerate(values[1:], 1):
        out = jnp.where(index == at, value, out)
    return out


def proxied(source, dest, n):
    return (source == 0 and dest >= 2) or (source == n - 1 and dest <= n - 3)


def route_tables(n):
    now, later, incoming = [], [], []
    for z in range(n):
        others = sorted((d for d in range(n) if d != z), key=lambda d: -abs(d - z))
        relay = {d for d in others if (z == 1 and proxied(0, d, n)) or (z == n - 2 and proxied(n - 1, d, n))}
        now.append([d for d in others if d not in relay])
        later.append([d for d in others if d in relay])
        incoming.append([s for s in others[::-1] if not proxied(s, z, n)])
    return now, later, incoming


def padded(rows, fill):
    longest = max(map(len, rows))
    return [[row[j] if j < len(row) else fill(z) for z, row in enumerate(rows)] for j in range(longest)]


def split_level(level):
    high = level.astype(jnp.bfloat16).astype(jnp.float32)
    rest = level - high
    middle = rest.astype(jnp.bfloat16).astype(jnp.float32)
    low = rest - middle
    filler = jnp.zeros((TAIL - 3 * level.shape[0], level.shape[1]), jnp.float32)
    return jnp.concatenate([high, middle, low, filler], axis=0).astype(jnp.bfloat16)


def join_level(tail, count):
    tail = tail.astype(jnp.float32)
    return tail[:count] + tail[count : 2 * count] + tail[2 * count : 3 * count]


def layer(
    n_row, n_chip, early, scale, pairs, slope, x_in, gain_in, wq_in, wkv_in, wo_in, table_in, b_in, e_in, out_ref, *scratch
):
    scratch = list(scratch)
    chunks = x_in.shape[1] // (CHUNK_HEADS * (x_in.shape[1] // slope.shape[0]))
    q_all = [scratch.pop(0) for _ in range(chunks)]
    (
        x_buf, n_in, n_buf, wq_buf, wkv_buf, wo_buf, k_buf, v_buf, b_buf, e_all, bias, table,
        scores, o_slot, m_slot, s_slot, codes, lookup, sib_out, sib_in, mix_out, via_in, got_in, own_o, own_l, acc,
        load_sem, x_sem, e_sem, q_send, q_recv, pair_send, pair_recv,
        sib_send, sib_recv, mix_send, via_recv, got_recv,
    ) = scratch
    row, col = lax.axis_index("row"), lax.axis_index("col")
    chip, core = col // CORES, col % CORES
    n_col = n_chip * CORES
    tile, width = x_in.shape
    heads = slope.shape[0]
    dim = width // heads
    hc = CHUNK_HEADS
    cw = hc * dim
    slot_cap = e_in.shape[1]
    slots = n_row * slot_cap
    f32, bf16 = jnp.float32, jnp.bfloat16
    sibling = (row, chip * CORES + (1 - core))
    chip_at = lambda z: (row, z * CORES + core)
    targets = [target_of(row, k, n_row) for k in range(1, n_row)]
    sources = [source_of(row, k, n_row) for k in range(1, n_row)]

    def load(src, dst, spot):
        copy = pltpu.make_async_copy(src, dst, load_sem.at[spot])
        copy.start()
        return copy

    def remote(src, dst, send, recv, where):
        return pltpu.make_async_remote_copy(
            src_ref=src, dst_ref=dst, send_sem=send, recv_sem=recv, device_id=where, device_id_type=MESH
        )

    x_load = load(x_in, x_buf, 0)
    wq_load = load(wq_in, wq_buf, 1)
    barrier = pltpu.get_barrier_semaphore()
    partners = [chip_at(target_of(chip, k, n_chip)) for k in range(1, n_chip)]
    if n_chip & (n_chip - 1):
        partners = [chip_at((chip + k) % n_chip) for k in range(1, n_chip)]
    partners = partners + [sibling] + [(r, col) for r in targets]
    for where in partners:
        pl.semaphore_signal(barrier, inc=1, device_id=where, device_id_type=MESH)
    b_load = load(b_in, b_buf, 2)
    own_e = load(e_in.at[row], e_all.at[row], 3)
    wkv_load = load(wkv_in, wkv_buf, 4)
    wo_load = load(wo_in, wo_buf, 5)

    table[...] = jnp.zeros(table.shape, f32)
    table[:, : table_in.shape[1]] = table_in[...]
    o_slot[slots] = jnp.zeros(o_slot.shape[1:], f32)
    m_slot[slots] = jnp.full(m_slot.shape[1:], LOW_FLOOR, f32)
    s_slot[slots] = jnp.zeros(s_slot.shape[1:], f32)

    x_load.wait()
    n_in[...] = normalize(x_buf[...], gain_in[...])
    pl.semaphore_wait(barrier, len(partners))

    x_copies = [
        remote(n_in, n_buf.at[k], x_sem.at[0, k], x_sem.at[1, k], (targets[k], col)) for k in range(n_row - 1)
    ]
    e_copies = [
        remote(e_in.at[targets[k]], e_all.at[row], e_sem.at[0, k], e_sem.at[1, k], (targets[k], col))
        for k in range(n_row - 1)
    ]
    for copy in x_copies + e_copies:
        copy.start()

    def e_arrival(k):
        there = e_all.at[sources[k]]
        return remote(there, there, e_sem.at[0, k], e_sem.at[1, k], (targets[k], col))

    def q_copy(c, k):
        here = q_all[c].at[col]
        return remote(here, here, q_send.at[c, k], q_recv.at[c, k], chip_at(target_of(chip, k + 1, n_chip)))

    def q_arrival(c, k):
        there = q_all[c].at[source_of(chip, k + 1, n_chip) * CORES + core]
        return remote(there, there, q_send.at[c, k], q_recv.at[c, k], sibling)

    def pair_copy(c, k, mine):
        origin = source_of(chip, k, n_chip) if k else chip
        there = q_all[c].at[origin * CORES + (core if mine else 1 - core)]
        return remote(there, there, pair_send.at[c, k], pair_recv.at[c, k], sibling)

    wq_load.wait()
    for c in range(chunks):
        cols = slice(c * cw, (c + 1) * cw)
        q_all[c][col] = jnp.dot(n_in[...], wq_buf[:, cols], preferred_element_type=f32).astype(bf16)
        for k in reversed(range(n_chip - 1)):
            q_copy(c, k).start()
        pair_copy(c, 0, True).start()

    @pl.loop(0, slots)
    def _(v):
        codes[v] = jnp.where(pairs[0, v] >= 0, pairs[0, v] * n_row + pairs[1, v] + v // slot_cap, -1)

    @pl.loop(0, n_col * n_row)
    def _(spot):
        found = jnp.int32(slots)
        for v in range(slots):
            found = jnp.where(codes[v] == spot, v, found)
        lookup[spot] = found

    def make_bias(owner, first, count):
        def one(k, carry):
            slot = owner * slot_cap + k
            buckets = b_buf[slot].T
            edges = e_all[owner, k].astype(f32).T
            for j in range(count):
                h = first + j
                entries = jnp.broadcast_to(table[h : h + 1, :], (tile, tile))
                picked = jnp.take_along_axis(entries, buckets, axis=1, mode="promise_in_bounds")
                bias[slot, j] = picked + slope[h] * edges
            return carry

        lax.fori_loop(0, slot_cap, one, 0)

    step = min(2 * LANES, width)

    def project(rows_ref, spot):
        hidden = rows_ref[...]

        @pl.loop(0, width // step)
        def _(at):
            left = pl.multiple_of(at * step, step)
            k_buf[spot, :, pl.ds(left, step)] = jnp.dot(
                hidden, wkv_buf[:, pl.ds(left, step)], preferred_element_type=f32
            ).astype(bf16)
            right = pl.multiple_of(width + left, step)
            value = jnp.dot(hidden, wkv_buf[:, pl.ds(right, step)], preferred_element_type=f32)
            v_buf[spot, pl.ds(left, step), :] = value.T.astype(bf16)

    def forward(c):
        for k in range(n_chip - 1):
            q_arrival(c, k).wait_recv()
            pair_copy(c, k + 1, True).start()

    b_load.wait()
    own_e.wait()
    if early:
        make_bias(row, 0, heads)
    wkv_load.wait()
    project(n_in, row)
    for k in range(n_row - 1):
        x_copies[k].wait_recv()
        project(n_buf.at[k], sources[k])
    forward(0)
    for k in range(n_row - 1):
        e_arrival(k).wait_recv()
        if early:
            make_bias(sources[k], 0, heads)

    group = slot_cap

    def attend(c):
        if not early:
            for r in range(n_row):
                make_bias(r, c * hc, hc)

        def one(t, carry):
            units = []
            for k in range(group):
                v = t * group + k
                query = jnp.maximum(pairs[0, v], 0)
                key = pairs[1, v] + v // slot_cap
                for j in range(hc):
                    h = c * hc + j
                    score = lax.dot_general(
                        k_buf[key, :, h * dim : (h + 1) * dim],
                        q_all[c][query, :, j * dim : (j + 1) * dim],
                        (((1,), (1,)), ((), ())),
                        preferred_element_type=f32,
                    )
                    score = score * scale + bias[v, h if early else j]
                    scores[k * hc + j] = score
                    units.append((v, key, h, j, jnp.max(score, axis=0, keepdims=True)))
            tops, sums = [], []
            for at, (v, key, h, j, top) in enumerate(units):
                probs = jnp.exp(scores[at] - top).astype(bf16)
                tops.append(top)
                sums.append(jnp.sum(probs.astype(f32), axis=0, keepdims=True))
                o_slot[v, j * dim : (j + 1) * dim, :] = jnp.dot(
                    v_buf[key, h * dim : (h + 1) * dim, :], probs, preferred_element_type=f32
                )
            for k in range(group):
                m_slot[t * group + k] = jnp.concatenate(tops[k * hc : (k + 1) * hc], axis=0)
                s_slot[t * group + k] = jnp.concatenate(sums[k * hc : (k + 1) * hc], axis=0)
            return carry

        lax.fori_loop(0, slots // group, one, 0)

    def combine(levels, weights_of, parts):
        top = functools.reduce(jnp.maximum, levels)
        shares = [jnp.exp(level - top) for level in levels]
        total = functools.reduce(jnp.add, [s if w is None else s * w for s, w in zip(shares, weights_of)])
        live = total > 0.0
        safe = jnp.where(live, total, 1.0)
        level = jnp.where(live, top + jnp.log(safe), LOW_FLOOR)
        inverse = 1.0 / safe
        shares = [share * inverse for share in shares]
        out = []
        for j in range(hc):
            rows = slice(j * dim, (j + 1) * dim)
            out.append(
                functools.reduce(jnp.add, [s[j : j + 1] * part(rows).astype(f32) for s, part in zip(shares, parts)])
            )
        return out, level

    def reader(ref):
        return lambda rows: ref[rows, :]

    def merge(block, extras):
        levels, weights, parts = [], [], []
        for r in range(n_row):
            v = lookup[block * n_row + r]
            levels.append(m_slot[v])
            weights.append(s_slot[v])
            parts.append(functools.partial(lambda v, rows: o_slot[v, rows, :], v))
        for ref in extras:
            levels.append(join_level(ref[cw : cw + TAIL, :], hc))
            weights.append(None)
            parts.append(reader(ref))
        return combine(levels, weights, parts)

    def put(ref, out, level):
        for j in range(hc):
            ref[j * dim : (j + 1) * dim, :] = out[j].astype(bf16)
        ref[cw : cw + TAIL, :] = split_level(level)

    now, later, incoming = route_tables(n_chip)
    now_at = padded(now, lambda z: z)
    later_at = padded(later, lambda z: z) if any(later) else []
    from_at = padded(incoming, lambda z: z)

    def sib_copy(c, z, mine):
        return remote(sib_out.at[c, z], sib_in.at[c, z], sib_send.at[c, z], sib_recv.at[c, z], sibling)

    def far_order():
        return [pick(chip, [sorted(range(n_chip), key=lambda d: -abs(d - z))[j] for z in range(n_chip)]) for j in range(n_chip)]

    order = far_order()

    def to_sibling(c):
        for z in order:
            put(sib_out.at[c, z], *merge(z * CORES + (1 - core), []))
            sib_copy(c, z, True).start()

    def direct(c, z):
        return remote(mix_out.at[c, z], got_in.at[c, chip], mix_send.at[c, z], got_recv.at[c, chip], chip_at(z))

    def got_from(c, s):
        return remote(mix_out.at[c, s], got_in.at[c, s], mix_send.at[c, s], got_recv.at[c, s], chip_at(s))

    def to_proxy(c, z):
        where = pick(chip, [1 if at == 0 else n_chip - 2 for at in range(n_chip)])
        return remote(mix_out.at[c, z], via_in.at[c, z], mix_send.at[c, z], via_recv.at[c, z], chip_at(where))

    def flags(rows):
        return [[1 if j < len(row) else 0 for row in rows] for j in range(max(map(len, rows)))]

    now_flags, later_flags, from_flags = flags(now), flags(later), flags(incoming)

    def guard(values, run):
        if all(values):
            run()
        elif any(values):
            pl.when(pick(chip, values) == 1)(run)

    def send_now(c):
        for j, dests in enumerate(now_at):
            z = pick(chip, dests)
            passes = [int(f and proxied(at, d, n_chip)) for at, (f, d) in enumerate(zip(now_flags[j], dests))]
            straight = [int(f and not proxied(at, d, n_chip)) for at, (f, d) in enumerate(zip(now_flags[j], dests))]

            def run(z=z, passes=passes, straight=straight):
                sib_copy(c, z, False).wait_recv()
                put(mix_out.at[c, z], *merge(z * CORES + core, [sib_in.at[c, z]]))
                guard(passes, lambda: to_proxy(c, z).start())
                guard(straight, lambda: direct(c, z).start())

            guard(now_flags[j], run)
        sib_copy(c, chip, False).wait_recv()
        out, level = merge(chip * CORES + core, [sib_in.at[c, chip]])
        for j in range(hc):
            own_o[c, j * dim : (j + 1) * dim, :] = out[j]
        own_l[c] = level

    def send_later(c):
        for j, dests in enumerate(later_at):
            z = pick(chip, dests)

            def run(z=z):
                sib_copy(c, z, False).wait_recv()
                to_proxy(c, z).wait_recv()
                put(mix_out.at[c, z], *merge(z * CORES + core, [sib_in.at[c, z], via_in.at[c, z]]))
                direct(c, z).start()

            guard(later_flags[j], run)

    for j, origins in enumerate(from_at):
        if not all(from_flags[j]):
            s = pick(chip, origins)

            def blank(s=s):
                for c in range(chunks):
                    got_in[c, s, :cw, :] = jnp.zeros((cw, tile), bf16)
                    got_in[c, s, cw:, :] = split_level(jnp.full((hc, tile), LOW_FLOOR, f32))

            guard([1 - f for f in from_flags[j]], blank)

    def finish(c):
        levels, parts = [own_l[c]], [lambda rows: own_o[c, rows, :]]
        for j, origins in enumerate(from_at):
            s = pick(chip, origins)
            guard(from_flags[j], lambda: got_from(c, s).wait_recv())
            ref = got_in.at[c, s]
            levels.append(join_level(ref[cw : cw + TAIL, :], hc))
            parts.append(reader(ref))
        out, _ = combine(levels, [None] * len(levels), parts)
        attention = jnp.concatenate([o.astype(bf16) for o in out], axis=0)
        update = lax.dot_general(
            attention, wo_buf[c * cw : (c + 1) * cw, :], (((0,), (0,)), ((), ())), preferred_element_type=f32
        )
        if c == 0:
            acc[...] = x_buf[...].astype(f32) + update
        elif c < chunks - 1:
            acc[...] += update
        else:
            out_ref[...] = (acc[...] + update).astype(out_ref.dtype)

    wo_load.wait()
    for c in range(chunks):
        for k in range(n_chip):
            pair_copy(c, k, False).wait_recv()
        if c + 1 < chunks:
            forward(c + 1)
        attend(c)
        to_sibling(c)
        send_now(c)
        send_later(c)
        if c:
            finish(c - 1)
    finish(chunks - 1)

    for copy in x_copies + e_copies:
        copy.wait_send()
    for c in range(chunks):
        for k in range(n_chip - 1):
            q_copy(c, k).wait_send()
        for k in range(n_chip):
            pair_copy(c, k, True).wait_send()
            sib_copy(c, k, True).wait_send()
        for k in range(n_chip - 1):
            z = target_of(chip, k + 1, n_chip)
            direct(c, z).wait_send()


def local(
    n_row,
    n_col,
    node_features,
    norm_gain,
    w_query,
    w_keyvalue,
    w_out,
    bias_table,
    edge_slope,
    pair_blocks,
    bucket_ids,
    edge_weight,
):
    tile, width = node_features.shape
    heads = edge_slope.shape[0]
    dim = width // heads
    n_chip = n_col // CORES
    slot_cap = edge_weight.shape[3]
    slots = n_row * slot_cap
    hc = CHUNK_HEADS
    cw = hc * dim
    chunks = heads // hc
    bf16, f32 = jnp.bfloat16, jnp.float32
    vmem = pl.BlockSpec(memory_space=pltpu.VMEM)
    smem = pl.BlockSpec(memory_space=pltpu.SMEM)
    hbm = pl.BlockSpec(memory_space=pl.ANY)
    early = 4 * slots * heads * tile * tile <= EARLY_BYTES
    message = (chunks, n_chip, cw + TAIL, tile)
    dma = pltpu.SemaphoreType.DMA
    scratch = [pltpu.VMEM((n_col, tile, cw), bf16)] * chunks + [
        pltpu.VMEM((tile, width), bf16),
        pltpu.VMEM((tile, width), bf16),
        pltpu.VMEM((n_row - 1, tile, width), bf16),
        pltpu.VMEM(w_query.shape, bf16),
        pltpu.VMEM(w_keyvalue.shape, bf16),
        pltpu.VMEM(w_out.shape, bf16),
        pltpu.VMEM((n_row, tile, width), bf16),
        pltpu.VMEM((n_row, width, tile), bf16),
        pltpu.VMEM((slots, tile, tile), jnp.int32),
        pltpu.VMEM((n_row,) + edge_weight.shape[3:], bf16),
        pltpu.VMEM((slots, heads if early else hc, tile, tile), f32),
        pltpu.VMEM((heads, tile), f32),
        pltpu.VMEM((slot_cap * hc, tile, tile), f32),
        pltpu.VMEM((slots + 1, cw, tile), f32),
        pltpu.VMEM((slots + 1, hc, tile), f32),
        pltpu.VMEM((slots + 1, hc, tile), f32),
        pltpu.SMEM((slots,), jnp.int32),
        pltpu.SMEM((n_col * n_row,), jnp.int32),
        pltpu.VMEM(message, bf16),
        pltpu.VMEM(message, bf16),
        pltpu.VMEM(message, bf16),
        pltpu.VMEM(message, bf16),
        pltpu.VMEM(message, bf16),
        pltpu.VMEM((chunks, cw, tile), f32),
        pltpu.VMEM((chunks, hc, tile), f32),
        pltpu.VMEM((tile, width), f32),
        dma((6,)),
        dma((2, n_row - 1)),
        dma((2, n_row - 1)),
        dma((chunks, n_chip - 1)),
        dma((chunks, n_chip - 1)),
        dma((chunks, n_chip)),
        dma((chunks, n_chip)),
        dma((chunks, n_chip)),
        dma((chunks, n_chip)),
        dma((chunks, n_chip)),
        dma((chunks, n_chip)),
        dma((chunks, n_chip)),
    ]
    return pl.pallas_call(
        functools.partial(layer, n_row, n_chip, early, dim ** (-0.5)),
        out_shape=jax.ShapeDtypeStruct((tile, width), bf16),
        in_specs=[smem, smem, hbm, vmem, hbm, hbm, hbm, vmem, hbm, hbm],
        out_specs=vmem,
        scratch_shapes=scratch,
        compiler_params=pltpu.CompilerParams(collective_id=0, has_side_effects=True, vmem_limit_bytes=VMEM_BYTES),
        name="layer",
    )(
        pair_blocks.reshape(2, slots),
        edge_slope,
        node_features,
        norm_gain[None],
        w_query,
        w_keyvalue,
        w_out,
        bias_table.T,
        bucket_ids.reshape(slots, tile, tile),
        edge_weight[0, 0],
    )


def solution(mesh):
    return jax.shard_map(
        functools.partial(local, mesh.shape["row"], mesh.shape["col"]),
        mesh=mesh,
        in_specs=(
            P(("row", "col"), None),
            P(),
            P(),
            P(),
            P(),
            P(),
            P(),
            P("row", "col", None, None),
            P("row", "col", None, None, None),
            P("row", "col", None, None, None, None),
        ),
        out_specs=P(("row", "col"), None),
        check_vma=False,
    )
```

```python
import functools

import jax
import jax.numpy as jnp
from jax import lax
from jax.experimental import pallas as pl
from jax.experimental.pallas import tpu as pltpu
from jax.sharding import PartitionSpec as P

EPSILON = 1e-05
LOW_FLOOR = -1e30
CORES = 2
MESH = pl.DeviceIdType.MESH
LANES = 128
CHUNK_HEADS = 2
TAIL = 8
EARLY_BYTES = 12 * 2**20
VMEM_BYTES = 67043328
SPARE = 0


def normalize(features, gain_vec):
    as_float = features.astype(jnp.float32)
    centered = as_float - jnp.mean(as_float, axis=-1, keepdims=True)
    variance = jnp.mean(centered * centered, axis=-1, keepdims=True)
    return (centered * lax.rsqrt(variance + EPSILON) * gain_vec).astype(jnp.bfloat16)


def target_of(index, k, n):
    if n & (n - 1):
        return (index + k) % n
    return index ^ k


def source_of(index, k, n):
    if n & (n - 1):
        return (index + n - k) % n
    return index ^ k


def pick(index, values):
    if all(v == values[0] for v in values):
        return values[0]
    out = values[0]
    for at, value in enumerate(values[1:], 1):
        out = jnp.where(index == at, value, out)
    return out


def proxied(source, dest, n):
    return (source == 0 and dest >= 2) or (source == n - 1 and dest <= n - 3)


def route_tables(n):
    now, later, incoming = [], [], []
    for z in range(n):
        others = sorted((d for d in range(n) if d != z), key=lambda d: -abs(d - z))
        relay = {d for d in others if (z == 1 and proxied(0, d, n)) or (z == n - 2 and proxied(n - 1, d, n))}
        now.append([d for d in others if d not in relay])
        later.append([d for d in others if d in relay])
        incoming.append([s for s in others[::-1] if not proxied(s, z, n)])
    return now, later, incoming


def padded(rows, fill):
    longest = max(map(len, rows))
    return [[row[j] if j < len(row) else fill(z) for z, row in enumerate(rows)] for j in range(longest)]


def split_level(level):
    high = level.astype(jnp.bfloat16).astype(jnp.float32)
    rest = level - high
    middle = rest.astype(jnp.bfloat16).astype(jnp.float32)
    low = rest - middle
    filler = jnp.zeros((TAIL - 3 * level.shape[0], level.shape[1]), jnp.float32)
    return jnp.concatenate([high, middle, low, filler], axis=0).astype(jnp.bfloat16)


def join_level(tail, count):
    tail = tail.astype(jnp.float32)
    return tail[:count] + tail[count : 2 * count] + tail[2 * count : 3 * count]


def layer(
    n_row, n_chip, early, scale, pairs, slope, x_in, gain_in, wq_in, wkv_in, wo_in, table_in, b_in, e_in, out_ref, *scratch
):
    scratch = list(scratch)
    chunks = x_in.shape[1] // (CHUNK_HEADS * (x_in.shape[1] // slope.shape[0]))
    q_all = [scratch.pop(0) for _ in range(chunks)]
    (
        x_buf, n_in, n_buf, wq_buf, wkv_buf, wo_buf, k_buf, v_buf, b_buf, e_all, bias, table,
        scores, o_slot, m_slot, s_slot, codes, lookup, sib_out, sib_in, mix_out, via_in, got_in, own_o, own_l,
        load_sem, x_sem, e_sem, q_send, q_recv, pair_send, pair_recv,
        sib_send, sib_recv, mix_send, via_recv, got_recv,
    ) = scratch
    row, col = lax.axis_index("row"), lax.axis_index("col")
    chip, core = col // CORES, col % CORES
    n_col = n_chip * CORES
    tile, width = x_in.shape
    heads = slope.shape[0]
    dim = width // heads
    hc = CHUNK_HEADS
    cw = hc * dim
    slot_cap = e_in.shape[1]
    slots = n_row * slot_cap
    f32, bf16 = jnp.float32, jnp.bfloat16
    sibling = (row, chip * CORES + (1 - core))
    chip_at = lambda z: (row, z * CORES + core)
    targets = [target_of(row, k, n_row) for k in range(1, n_row)]
    sources = [source_of(row, k, n_row) for k in range(1, n_row)]

    def load(src, dst, spot):
        copy = pltpu.make_async_copy(src, dst, load_sem.at[spot])
        copy.start()
        return copy

    def remote(src, dst, send, recv, where):
        return pltpu.make_async_remote_copy(
            src_ref=src, dst_ref=dst, send_sem=send, recv_sem=recv, device_id=where, device_id_type=MESH
        )

    x_load = load(x_in, x_buf, 0)
    wq_load = load(wq_in, wq_buf, 1)
    barrier = pltpu.get_barrier_semaphore()
    partners = [chip_at(target_of(chip, k, n_chip)) for k in range(1, n_chip)]
    if n_chip & (n_chip - 1):
        partners = [chip_at((chip + k) % n_chip) for k in range(1, n_chip)]
    partners = partners + [sibling] + [(r, col) for r in targets]
    for where in partners:
        pl.semaphore_signal(barrier, inc=1, device_id=where, device_id_type=MESH)
    b_load = load(b_in, b_buf, 2)
    own_e = load(e_in.at[row], e_all.at[row], 3)
    wkv_load = load(wkv_in, wkv_buf, 4)
    wo_load = load(wo_in, wo_buf, 5)

    table[...] = jnp.zeros(table.shape, f32)
    table[:, : table_in.shape[1]] = table_in[...]
    o_slot[slots] = jnp.zeros(o_slot.shape[1:], f32)
    m_slot[slots] = jnp.full(m_slot.shape[1:], LOW_FLOOR, f32)
    s_slot[slots] = jnp.zeros(s_slot.shape[1:], f32)

    relayed = n_row == 4
    direct_rows = range(n_row - 1 - relayed)
    half = width // 2
    sides = [slice(0, half), slice(half, width)]

    def e_copy(k):
        return remote(e_in.at[targets[k]], e_all.at[row], e_sem.at[0, k], e_sem.at[1, k], (targets[k], col))

    def e_arrival(k):
        there = e_all.at[sources[k]]
        return remote(there, there, e_sem.at[0, k], e_sem.at[1, k], (targets[k], col))

    def x_copy(k):
        return remote(n_in, n_buf.at[k], x_sem.at[0, k], x_sem.at[1, k], (targets[k], col))

    def relay_copy(side):
        part = n_buf.at[1 - side, :, sides[side]]
        there = n_buf.at[n_row - 2, :, sides[side]]
        spot = n_row - 1 + side
        return remote(part, there, x_sem.at[0, spot], x_sem.at[1, spot], (targets[side], col))

    def line_copy(c, step, way):
        there = q_all[c].at[(chip - way * step) * CORES + core]
        origin = chip - way * step
        return remote(there, there, q_send.at[c, step, (way + 1) // 2], q_recv.at[c, origin], chip_at(chip + way))

    def line_arrival(c, step, way):
        origin = chip - way * step
        there = q_all[c].at[origin * CORES + core]
        return remote(there, there, q_send.at[c, step, (way + 1) // 2], q_recv.at[c, origin], sibling)

    def pair_copy(c, origin, mine):
        there = q_all[c].at[origin * CORES + (core if mine else 1 - core)]
        return remote(there, there, pair_send.at[c, origin], pair_recv.at[c, origin], sibling)

    def inside(z):
        return (z >= 0) & (z < n_chip)

    def send_own(c):
        for way in (1, -1):
            pl.when(inside(chip + way))(lambda: line_copy(c, 0, way).start())
        pair_copy(c, chip, True).start()

    def wave(w):
        for c in range(chunks):
            step = w - c + 1
            if not 1 <= step < n_chip:
                continue
            for way in (1, -1):
                origin = chip - way * step

                @pl.when(inside(origin))
                def _():
                    line_arrival(c, step, way).wait_recv()
                    if step < n_chip - 1:
                        pl.when(inside(chip + way))(lambda: line_copy(c, step, way).start())
                    pair_copy(c, origin, True).start()

        if w + 2 < chunks:
            send_own(w + 2)

    waves = list(range(chunks + n_chip - 2))

    def next_wave():
        if waves:
            wave(waves.pop(0))

    x_load.wait()
    n_in[...] = normalize(x_buf[...], gain_in[...])
    pl.semaphore_wait(barrier, len(partners))
    for k in direct_rows:
        x_copy(k).start()
    for k in range(n_row - 1):
        e_copy(k).start()
    wq_load.wait()
    for c in range(chunks):
        cols = slice(c * cw, (c + 1) * cw)
        q_all[c][col] = jnp.dot(n_in[...], wq_buf[:, cols], preferred_element_type=f32).astype(bf16)
        if c < 2:
            send_own(c)

    @pl.loop(0, slots)
    def _(v):
        codes[v] = jnp.where(pairs[0, v] >= 0, pairs[0, v] * n_row + pairs[1, v] + v // slot_cap, -1)

    @pl.loop(0, n_col * n_row)
    def _(spot):
        found = jnp.int32(slots)
        for v in range(slots):
            found = jnp.where(codes[v] == spot, v, found)
        lookup[spot] = found

    def make_bias(owner, first, count, buckets_too=True, edges_too=True):
        def one(k, carry):
            slot = owner * slot_cap + k
            if buckets_too:
                buckets = b_buf[slot].T
            if edges_too:
                edges = e_all[owner, k].astype(f32).T
            for j in range(count):
                h = first + j
                if buckets_too:
                    entries = jnp.broadcast_to(table[h : h + 1, :], (tile, tile))
                    term = jnp.take_along_axis(entries, buckets, axis=1, mode="promise_in_bounds")
                else:
                    term = bias[slot, j]
                bias[slot, j] = term + slope[h] * edges if edges_too else term
            return carry

        lax.fori_loop(0, slot_cap, one, 0)

    step = min(2 * LANES, width)

    def project(rows_ref, spot):
        hidden = rows_ref[...]

        @pl.loop(0, width // step)
        def _(at):
            left = pl.multiple_of(at * step, step)
            k_buf[spot, :, pl.ds(left, step)] = jnp.dot(
                hidden, wkv_buf[:, pl.ds(left, step)], preferred_element_type=f32
            ).astype(bf16)
            right = pl.multiple_of(width + left, step)
            value = jnp.dot(hidden, wkv_buf[:, pl.ds(right, step)], preferred_element_type=f32)
            v_buf[spot, pl.ds(left, step), :] = value.T.astype(bf16)

    ahead = min(2, n_row - 1)
    b_load.wait()
    own_e.wait()
    wkv_load.wait()
    project(n_in, row)
    if early:
        make_bias(row, 0, heads)
    next_wave()
    if early:
        for k in range(ahead):
            make_bias(sources[k], 0, heads, edges_too=False)
    for k in direct_rows:
        x_copy(k).wait_recv()
        if relayed:
            relay_copy(1 - k).start()
    next_wave()
    for k in direct_rows:
        project(n_buf.at[k], sources[k])
    for k in range(n_row - 1):
        e_arrival(k).wait_recv()
        if early:
            make_bias(sources[k], 0, heads, buckets_too=k >= ahead)
        if k == 1 or k == n_row - 2:
            next_wave()
    if relayed:
        for side in range(2):
            relay_copy(side).wait_recv()
        project(n_buf.at[n_row - 2], sources[n_row - 2])

    group = slot_cap

    def attend(c):
        if not early:
            for r in range(n_row):
                make_bias(r, c * hc, hc)

        def one(t, carry):
            units = []
            for k in range(group):
                v = t * group + k
                query = jnp.maximum(pairs[0, v], 0)
                key = pairs[1, v] + v // slot_cap
                for j in range(hc):
                    h = c * hc + j
                    score = lax.dot_general(
                        k_buf[key, :, h * dim : (h + 1) * dim],
                        q_all[c][query, :, j * dim : (j + 1) * dim],
                        (((1,), (1,)), ((), ())),
                        preferred_element_type=f32,
                    )
                    score = score * scale + bias[v, h if early else j]
                    scores[k * hc + j] = score
                    units.append((v, key, h, j, jnp.max(score, axis=0, keepdims=True)))
            tops, sums = [], []
            for at, (v, key, h, j, top) in enumerate(units):
                probs = jnp.exp(scores[at] - top).astype(bf16)
                tops.append(top)
                sums.append(jnp.sum(probs.astype(f32), axis=0, keepdims=True))
                o_slot[v, j * dim : (j + 1) * dim, :] = jnp.dot(
                    v_buf[key, h * dim : (h + 1) * dim, :], probs, preferred_element_type=f32
                )
            for k in range(group):
                m_slot[t * group + k] = jnp.concatenate(tops[k * hc : (k + 1) * hc], axis=0)
                s_slot[t * group + k] = jnp.concatenate(sums[k * hc : (k + 1) * hc], axis=0)
            return carry

        lax.fori_loop(0, slots // group, one, 0)

    def combine(levels, weights_of, parts):
        top = functools.reduce(jnp.maximum, levels)
        shares = [jnp.exp(level - top) for level in levels]
        total = functools.reduce(jnp.add, [s if w is None else s * w for s, w in zip(shares, weights_of)])
        live = total > 0.0
        safe = jnp.where(live, total, 1.0)
        level = jnp.where(live, top + jnp.log(safe), LOW_FLOOR)
        inverse = 1.0 / safe
        shares = [share * inverse for share in shares]
        out = []
        for j in range(hc):
            rows = slice(j * dim, (j + 1) * dim)
            out.append(
                functools.reduce(jnp.add, [s[j : j + 1] * part(rows).astype(f32) for s, part in zip(shares, parts)])
            )
        return out, level

    def reader(ref):
        return lambda rows: ref[rows, :]

    def merge(block, extras):
        levels, weights, parts = [], [], []
        for r in range(n_row):
            v = lookup[block * n_row + r]
            levels.append(m_slot[v])
            weights.append(s_slot[v])
            parts.append(functools.partial(lambda v, rows: o_slot[v, rows, :], v))
        for ref in extras:
            levels.append(join_level(ref[cw : cw + TAIL, :], hc))
            weights.append(None)
            parts.append(reader(ref))
        return combine(levels, weights, parts)

    def put(ref, out, level):
        for j in range(hc):
            ref[j * dim : (j + 1) * dim, :] = out[j].astype(bf16)
        ref[cw : cw + TAIL, :] = split_level(level)

    now, later, incoming = route_tables(n_chip)
    now_at = padded(now, lambda z: z)
    later_at = padded(later, lambda z: z) if any(later) else []
    from_at = padded(incoming, lambda z: z)

    def sib_copy(c, z, mine):
        return remote(sib_out.at[c, z], sib_in.at[c, z], sib_send.at[c, z], sib_recv.at[c, z], sibling)

    def far_order():
        return [pick(chip, [sorted(range(n_chip), key=lambda d: -abs(d - z))[j] for z in range(n_chip)]) for j in range(n_chip)]

    order = far_order()

    def to_sibling(c):
        for z in order:
            put(sib_out.at[c, z], *merge(z * CORES + (1 - core), []))
            sib_copy(c, z, True).start()

    def direct(c, z):
        return remote(mix_out.at[c, z], got_in.at[c, chip], mix_send.at[c, z], got_recv.at[c, chip], chip_at(z))

    def got_from(c, s):
        return remote(mix_out.at[c, s], got_in.at[c, s], mix_send.at[c, s], got_recv.at[c, s], chip_at(s))

    def to_proxy(c, z):
        where = pick(chip, [1 if at == 0 else n_chip - 2 for at in range(n_chip)])
        return remote(mix_out.at[c, z], via_in.at[c, z], mix_send.at[c, z], via_recv.at[c, z], chip_at(where))

    def flags(rows):
        return [[1 if j < len(row) else 0 for row in rows] for j in range(max(map(len, rows)))]

    now_flags, later_flags, from_flags = flags(now), flags(later), flags(incoming)

    def guard(values, run):
        if all(values):
            run()
        elif any(values):
            pl.when(pick(chip, values) == 1)(run)

    def send_now(c):
        for j, dests in enumerate(now_at):
            z = pick(chip, dests)
            passes = [int(f and proxied(at, d, n_chip)) for at, (f, d) in enumerate(zip(now_flags[j], dests))]
            straight = [int(f and not proxied(at, d, n_chip)) for at, (f, d) in enumerate(zip(now_flags[j], dests))]

            def run(z=z, passes=passes, straight=straight):
                sib_copy(c, z, False).wait_recv()
                put(mix_out.at[c, z], *merge(z * CORES + core, [sib_in.at[c, z]]))
                guard(passes, lambda: to_proxy(c, z).start())
                guard(straight, lambda: direct(c, z).start())

            guard(now_flags[j], run)
        sib_copy(c, chip, False).wait_recv()
        out, level = merge(chip * CORES + core, [sib_in.at[c, chip]])
        for j in range(hc):
            own_o[c, j * dim : (j + 1) * dim, :] = out[j]
        own_l[c] = level

    def hold(c):
        for j, dests in enumerate(later_at):
            z = pick(chip, dests)

            def run(z=z):
                sib_copy(c, z, False).wait_recv()
                put(mix_out.at[c, z], *merge(z * CORES + core, [sib_in.at[c, z]]))

            guard(later_flags[j], run)

    def send_later(c):
        for j, dests in enumerate(later_at):
            z = pick(chip, dests)

            def run(z=z):
                to_proxy(c, z).wait_recv()
                refs = [mix_out.at[c, z], via_in.at[c, z]]
                levels = [join_level(ref[cw : cw + TAIL, :], hc) for ref in refs]
                put(mix_out.at[c, z], *combine(levels, [None] * 2, [reader(ref) for ref in refs]))
                direct(c, z).start()

            guard(later_flags[j], run)

    for j, origins in enumerate(from_at):
        if not all(from_flags[j]):
            s = pick(chip, origins)

            def blank(s=s):
                for c in range(chunks):
                    got_in[c, s, :cw, :] = jnp.zeros((cw, tile), bf16)
                    got_in[c, s, cw:, :] = split_level(jnp.full((hc, tile), LOW_FLOOR, f32))

            guard([1 - f for f in from_flags[j]], blank)

    def finish(c):
        levels, parts = [own_l[c]], [lambda rows: own_o[c, rows, :]]
        for j, origins in enumerate(from_at):
            s = pick(chip, origins)
            guard(from_flags[j], lambda: got_from(c, s).wait_recv())
            ref = got_in.at[c, s]
            levels.append(join_level(ref[cw : cw + TAIL, :], hc))
            parts.append(reader(ref))
        out, _ = combine(levels, [None] * len(levels), parts)
        attention = jnp.concatenate([o.astype(bf16) for o in out], axis=0)
        update = lax.dot_general(
            attention, wo_buf[c * cw : (c + 1) * cw, :], (((0,), (0,)), ((), ())), preferred_element_type=f32
        )
        if c == 0:
            out_ref[...] = update
        else:
            out_ref[...] += update

    wo_load.wait()
    for c in range(chunks):
        while waves and waves[0] < c + n_chip - 1:
            next_wave()
        for z in range(n_chip):
            pair_copy(c, z, False).wait_recv()
        attend(c)
        next_wave()
        to_sibling(c)
        send_now(c)
        hold(c)
        if c:
            send_later(c - 1)
        if c > 1:
            finish(c - 2)
    send_later(chunks - 1)
    for c in range(max(chunks - 2, 0), chunks):
        finish(c)

    for k in range(n_row - 1):
        e_copy(k).wait_send()
    for k in direct_rows:
        x_copy(k).wait_send()
    if relayed:
        for side in range(2):
            relay_copy(side).wait_send()
    for c in range(chunks):
        for way in (1, -1):
            for step in range(n_chip - 1):
                pl.when(inside(chip + way) & inside(chip - way * step))(lambda: line_copy(c, step, way).wait_send())
        for z in range(n_chip):
            pair_copy(c, z, True).wait_send()
            sib_copy(c, z, True).wait_send()
        for k in range(n_chip - 1):
            direct(c, target_of(chip, k + 1, n_chip)).wait_send()


def local(
    n_row,
    n_col,
    node_features,
    norm_gain,
    w_query,
    w_keyvalue,
    w_out,
    bias_table,
    edge_slope,
    pair_blocks,
    bucket_ids,
    edge_weight,
):
    tile, width = node_features.shape
    heads = edge_slope.shape[0]
    dim = width // heads
    n_chip = n_col // CORES
    slot_cap = edge_weight.shape[3]
    slots = n_row * slot_cap
    hc = CHUNK_HEADS
    cw = hc * dim
    chunks = heads // hc
    bf16, f32 = jnp.bfloat16, jnp.float32
    vmem = pl.BlockSpec(memory_space=pltpu.VMEM)
    smem = pl.BlockSpec(memory_space=pltpu.SMEM)
    hbm = pl.BlockSpec(memory_space=pltpu.HBM)
    early = 4 * slots * heads * tile * tile <= EARLY_BYTES
    message = (chunks, n_chip, cw + TAIL, tile)
    dma = pltpu.SemaphoreType.DMA
    scratch = [pltpu.VMEM((n_col, tile, cw), bf16)] * chunks + [
        pltpu.VMEM((tile, width), bf16),
        pltpu.VMEM((tile, width), bf16),
        pltpu.VMEM((n_row - 1, tile, width), bf16),
        pltpu.VMEM(w_query.shape, bf16),
        pltpu.VMEM(w_keyvalue.shape, bf16),
        pltpu.VMEM(w_out.shape, bf16),
        pltpu.VMEM((n_row, tile, width), bf16),
        pltpu.VMEM((n_row, width, tile), bf16),
        pltpu.VMEM((slots, tile, tile), jnp.int32),
        pltpu.VMEM((n_row,) + edge_weight.shape[3:], bf16),
        pltpu.VMEM((slots, heads if early else hc, tile, tile), f32),
        pltpu.VMEM((heads, tile), f32),
        pltpu.VMEM((slot_cap * hc, tile, tile), f32),
        pltpu.VMEM((slots + 1, cw, tile), f32),
        pltpu.VMEM((slots + 1, hc, tile), f32),
        pltpu.VMEM((slots + 1, hc, tile), f32),
        pltpu.SMEM((slots,), jnp.int32),
        pltpu.SMEM((n_col * n_row,), jnp.int32),
        pltpu.VMEM(message, bf16),
        pltpu.VMEM(message, bf16),
        pltpu.VMEM(message, bf16),
        pltpu.VMEM(message, bf16),
        pltpu.VMEM(message, bf16),
        pltpu.VMEM((chunks, cw, tile), f32),
        pltpu.VMEM((chunks, hc, tile), f32),
        dma((6,)),
        dma((2, n_row + 1)),
        dma((2, n_row - 1)),
        dma((chunks, n_chip - 1, 2)),
        dma((chunks, n_chip)),
        dma((chunks, n_chip)),
        dma((chunks, n_chip)),
        dma((chunks, n_chip)),
        dma((chunks, n_chip)),
        dma((chunks, n_chip)),
        dma((chunks, n_chip)),
        dma((chunks, n_chip)),
    ]
    update = pl.pallas_call(
        functools.partial(layer, n_row, n_chip, early, dim ** (-0.5)),
        out_shape=jax.ShapeDtypeStruct((tile, width), f32),
        in_specs=[smem, smem, hbm, vmem, hbm, hbm, hbm, vmem, hbm, hbm],
        out_specs=vmem,
        scratch_shapes=scratch,
        compiler_params=pltpu.CompilerParams(collective_id=0, has_side_effects=True, vmem_limit_bytes=VMEM_BYTES - SPARE),
        name="layer",
    )(
        pair_blocks.reshape(2, slots),
        edge_slope,
        node_features,
        norm_gain[None],
        w_query,
        w_keyvalue,
        w_out,
        bias_table.T,
        bucket_ids.reshape(slots, tile, tile),
        edge_weight[0, 0],
    )
    return (node_features.astype(f32) + update).astype(bf16)


def solution(mesh):
    return jax.shard_map(
        functools.partial(local, mesh.shape["row"], mesh.shape["col"]),
        mesh=mesh,
        in_specs=(
            P(("row", "col"), None),
            P(),
            P(),
            P(),
            P(),
            P(),
            P(),
            P("row", "col", None, None),
            P("row", "col", None, None, None),
            P("row", "col", None, None, None, None),
        ),
        out_specs=P(("row", "col"), None),
        check_vma=False,
    )
```

```python
import functools

import jax
import jax.numpy as jnp
from jax import lax
from jax.experimental import pallas as pl
from jax.experimental.pallas import tpu as pltpu
from jax.sharding import PartitionSpec as P

EPSILON = 1e-05
LOW_FLOOR = -1e30
CORES = 2
MESH = pl.DeviceIdType.MESH
LANES = 128
CHUNK_HEADS = 2
TAIL = 8
EARLY_BYTES = 12 * 2**20
VMEM_BYTES = 67043328
SPARE = 0


def normalize(features, gain_vec):
    as_float = features.astype(jnp.float32)
    centered = as_float - jnp.mean(as_float, axis=-1, keepdims=True)
    variance = jnp.mean(centered * centered, axis=-1, keepdims=True)
    return (centered * lax.rsqrt(variance + EPSILON) * gain_vec).astype(jnp.bfloat16)


def target_of(index, k, n):
    if n & (n - 1):
        return (index + k) % n
    return index ^ k


def source_of(index, k, n):
    if n & (n - 1):
        return (index + n - k) % n
    return index ^ k


def pick(index, values):
    if all(v == values[0] for v in values):
        return values[0]
    out = values[0]
    for at, value in enumerate(values[1:], 1):
        out = jnp.where(index == at, value, out)
    return out


def proxied(source, dest, n):
    return (source == 0 and dest >= 2) or (source == n - 1 and dest <= n - 3)


def route_tables(n):
    now, later, incoming = [], [], []
    for z in range(n):
        others = sorted((d for d in range(n) if d != z), key=lambda d: -abs(d - z))
        relay = {d for d in others if (z == 1 and proxied(0, d, n)) or (z == n - 2 and proxied(n - 1, d, n))}
        now.append([d for d in others if d not in relay])
        later.append([d for d in others if d in relay])
        incoming.append([s for s in others[::-1] if not proxied(s, z, n)])
    return now, later, incoming


def padded(rows, fill):
    longest = max(map(len, rows))
    return [[row[j] if j < len(row) else fill(z) for z, row in enumerate(rows)] for j in range(longest)]


def split_level(level):
    high = level.astype(jnp.bfloat16).astype(jnp.float32)
    rest = level - high
    middle = rest.astype(jnp.bfloat16).astype(jnp.float32)
    low = rest - middle
    filler = jnp.zeros((TAIL - 3 * level.shape[0], level.shape[1]), jnp.float32)
    return jnp.concatenate([high, middle, low, filler], axis=0).astype(jnp.bfloat16)


def join_level(tail, count):
    tail = tail.astype(jnp.float32)
    return tail[:count] + tail[count : 2 * count] + tail[2 * count : 3 * count]


def layer(
    n_row, n_chip, early, scale, pairs, slope, x_in, gain_in, wq_in, wkv_in, wo_in, table_in, b_in, e_in, out_ref, *scratch
):
    scratch = list(scratch)
    chunks = x_in.shape[1] // (CHUNK_HEADS * (x_in.shape[1] // slope.shape[0]))
    q_all = [scratch.pop(0) for _ in range(chunks)]
    (
        x_buf, n_in, n_buf, wq_buf, wkv_buf, wo_buf, k_buf, v_buf, b_buf, e_all, bias, table,
        scores, o_slot, m_slot, s_slot, codes, lookup, sib_out, sib_in, mix_out, via_in, got_in, own_o, own_l,
        load_sem, x_sem, e_sem, q_send, q_recv, pair_send, pair_recv,
        sib_send, sib_recv, mix_send, via_recv, got_recv,
    ) = scratch
    row, col = lax.axis_index("row"), lax.axis_index("col")
    chip, core = col // CORES, col % CORES
    n_col = n_chip * CORES
    tile, width = x_in.shape
    heads = slope.shape[0]
    dim = width // heads
    hc = CHUNK_HEADS
    cw = hc * dim
    slot_cap = e_in.shape[1]
    slots = n_row * slot_cap
    f32, bf16 = jnp.float32, jnp.bfloat16
    sibling = (row, chip * CORES + (1 - core))
    chip_at = lambda z: (row, z * CORES + core)
    targets = [target_of(row, k, n_row) for k in range(1, n_row)]
    sources = [source_of(row, k, n_row) for k in range(1, n_row)]

    def load(src, dst, spot):
        copy = pltpu.make_async_copy(src, dst, load_sem.at[spot])
        copy.start()
        return copy

    def remote(src, dst, send, recv, where):
        return pltpu.make_async_remote_copy(
            src_ref=src, dst_ref=dst, send_sem=send, recv_sem=recv, device_id=where, device_id_type=MESH
        )

    x_load = load(x_in, x_buf, 0)
    wq_load = load(wq_in, wq_buf, 1)
    barrier = pltpu.get_barrier_semaphore()
    partners = [chip_at(target_of(chip, k, n_chip)) for k in range(1, n_chip)]
    if n_chip & (n_chip - 1):
        partners = [chip_at((chip + k) % n_chip) for k in range(1, n_chip)]
    partners = partners + [sibling] + [(r, col) for r in targets]
    for where in partners:
        pl.semaphore_signal(barrier, inc=1, device_id=where, device_id_type=MESH)
    b_load = load(b_in, b_buf, 2)
    own_e = load(e_in.at[row], e_all.at[row], 3)
    wkv_load = load(wkv_in, wkv_buf, 4)
    wo_load = load(wo_in, wo_buf, 5)

    table[...] = jnp.zeros(table.shape, f32)
    table[:, : table_in.shape[1]] = table_in[...]
    o_slot[slots] = jnp.zeros(o_slot.shape[1:], f32)
    m_slot[slots] = jnp.full(m_slot.shape[1:], LOW_FLOOR, f32)
    s_slot[slots] = jnp.zeros(s_slot.shape[1:], f32)

    relayed = n_row == 4
    direct_rows = range(n_row - 1 - relayed)
    half = width // 2
    sides = [slice(0, half), slice(half, width)]

    def e_copy(k):
        return remote(e_in.at[targets[k]], e_all.at[row], e_sem.at[0, k], e_sem.at[1, k], (targets[k], col))

    def e_arrival(k):
        there = e_all.at[sources[k]]
        return remote(there, there, e_sem.at[0, k], e_sem.at[1, k], (targets[k], col))

    def x_copy(k):
        return remote(n_in, n_buf.at[k], x_sem.at[0, k], x_sem.at[1, k], (targets[k], col))

    def relay_copy(side):
        part = n_buf.at[1 - side, :, sides[side]]
        there = n_buf.at[n_row - 2, :, sides[side]]
        spot = n_row - 1 + side
        return remote(part, there, x_sem.at[0, spot], x_sem.at[1, spot], (targets[side], col))

    def line_copy(c, step, way):
        there = q_all[c].at[(chip - way * step) * CORES + core]
        origin = chip - way * step
        return remote(there, there, q_send.at[c, step, (way + 1) // 2], q_recv.at[c, origin], chip_at(chip + way))

    def line_arrival(c, step, way):
        origin = chip - way * step
        there = q_all[c].at[origin * CORES + core]
        return remote(there, there, q_send.at[c, step, (way + 1) // 2], q_recv.at[c, origin], sibling)

    def pair_copy(c, origin, mine):
        there = q_all[c].at[origin * CORES + (core if mine else 1 - core)]
        return remote(there, there, pair_send.at[c, origin], pair_recv.at[c, origin], sibling)

    def inside(z):
        return (z >= 0) & (z < n_chip)

    def send_own(c):
        for way in (1, -1):
            pl.when(inside(chip + way))(lambda: line_copy(c, 0, way).start())
        pair_copy(c, chip, True).start()

    def wave(w):
        for c in range(chunks):
            step = w - c + 1
            if not 1 <= step < n_chip:
                continue
            for way in (1, -1):
                origin = chip - way * step

                @pl.when(inside(origin))
                def _():
                    line_arrival(c, step, way).wait_recv()
                    if step < n_chip - 1:
                        pl.when(inside(chip + way))(lambda: line_copy(c, step, way).start())
                    pair_copy(c, origin, True).start()

        if w + 2 < chunks:
            send_own(w + 2)

    waves = list(range(chunks + n_chip - 2))

    def next_wave():
        if waves:
            wave(waves.pop(0))

    x_load.wait()
    n_in[...] = normalize(x_buf[...], gain_in[...])
    pl.semaphore_wait(barrier, len(partners))
    for k in direct_rows:
        x_copy(k).start()
    for k in direct_rows:
        e_copy(k).start()
    wq_load.wait()
    for c in range(chunks):
        cols = slice(c * cw, (c + 1) * cw)
        q_all[c][col] = jnp.dot(n_in[...], wq_buf[:, cols], preferred_element_type=f32).astype(bf16)
        if c < 2:
            send_own(c)

    @pl.loop(0, slots)
    def _(v):
        codes[v] = jnp.where(pairs[0, v] >= 0, pairs[0, v] * n_row + pairs[1, v] + v // slot_cap, -1)

    @pl.loop(0, n_col * n_row)
    def _(spot):
        found = jnp.int32(slots)
        for v in range(slots):
            found = jnp.where(codes[v] == spot, v, found)
        lookup[spot] = found

    def make_bias(owner, first, count, buckets_too=True, edges_too=True):
        def one(k, carry):
            slot = owner * slot_cap + k
            if buckets_too:
                buckets = b_buf[slot].T
            if edges_too:
                edges = e_all[owner, k].astype(f32).T
            for j in range(count):
                h = first + j
                if buckets_too:
                    entries = jnp.broadcast_to(table[h : h + 1, :], (tile, tile))
                    term = jnp.take_along_axis(entries, buckets, axis=1, mode="promise_in_bounds")
                else:
                    term = bias[slot, j]
                bias[slot, j] = term + slope[h] * edges if edges_too else term
            return carry

        lax.fori_loop(0, slot_cap, one, 0)

    step = min(2 * LANES, width)

    def project(rows_ref, spot):
        hidden = rows_ref[...]

        @pl.loop(0, width // step)
        def _(at):
            left = pl.multiple_of(at * step, step)
            k_buf[spot, :, pl.ds(left, step)] = jnp.dot(
                hidden, wkv_buf[:, pl.ds(left, step)], preferred_element_type=f32
            ).astype(bf16)
            right = pl.multiple_of(width + left, step)
            value = jnp.dot(hidden, wkv_buf[:, pl.ds(right, step)], preferred_element_type=f32)
            v_buf[spot, pl.ds(left, step), :] = value.T.astype(bf16)

    ahead = min(2, n_row - 1)
    b_load.wait()
    own_e.wait()
    wkv_load.wait()
    project(n_in, row)
    if early:
        make_bias(row, 0, heads)
    next_wave()
    if early:
        for k in range(ahead):
            make_bias(sources[k], 0, heads, edges_too=False)
    for k in direct_rows:
        x_copy(k).wait_recv()
        if relayed:
            relay_copy(1 - k).start()
    if relayed:
        e_copy(n_row - 2).start()
    next_wave()
    for k in direct_rows:
        project(n_buf.at[k], sources[k])
    for k in direct_rows:
        e_arrival(k).wait_recv()
        if early:
            make_bias(sources[k], 0, heads, buckets_too=k >= ahead)
        if k == 1:
            next_wave()
    if relayed:
        if early:
            make_bias(sources[n_row - 2], 0, heads, edges_too=False)
        for side in range(2):
            relay_copy(side).wait_recv()
        project(n_buf.at[n_row - 2], sources[n_row - 2])
        next_wave()
        e_arrival(n_row - 2).wait_recv()
        if early:
            make_bias(sources[n_row - 2], 0, heads, buckets_too=False)
    else:
        next_wave()

    group = scores.shape[0] // hc

    def attend(c):
        if not early:
            for r in range(n_row):
                make_bias(r, c * hc, hc)

        def one(t, carry):
            units = []
            for k in range(group):
                v = t * group + k
                query = jnp.maximum(pairs[0, v], 0)
                key = pairs[1, v] + v // slot_cap
                for j in range(hc):
                    h = c * hc + j
                    score = lax.dot_general(
                        k_buf[key, :, h * dim : (h + 1) * dim],
                        q_all[c][query, :, j * dim : (j + 1) * dim],
                        (((1,), (1,)), ((), ())),
                        preferred_element_type=f32,
                    )
                    score = score * scale + bias[v, h if early else j]
                    scores[k * hc + j] = score
                    units.append((v, key, h, j, jnp.max(score, axis=0, keepdims=True)))
            tops, sums = [], []
            for at, (v, key, h, j, top) in enumerate(units):
                probs = jnp.exp(scores[at] - top).astype(bf16)
                tops.append(top)
                sums.append(jnp.sum(probs.astype(f32), axis=0, keepdims=True))
                o_slot[v, j * dim : (j + 1) * dim, :] = jnp.dot(
                    v_buf[key, h * dim : (h + 1) * dim, :], probs, preferred_element_type=f32
                )
            for k in range(group):
                m_slot[t * group + k] = jnp.concatenate(tops[k * hc : (k + 1) * hc], axis=0)
                s_slot[t * group + k] = jnp.concatenate(sums[k * hc : (k + 1) * hc], axis=0)
            return carry

        lax.fori_loop(0, slots // group, one, 0)

    def combine(levels, weights_of, parts):
        top = functools.reduce(jnp.maximum, levels)
        shares = [jnp.exp(level - top) for level in levels]
        total = functools.reduce(jnp.add, [s if w is None else s * w for s, w in zip(shares, weights_of)])
        live = total > 0.0
        safe = jnp.where(live, total, 1.0)
        level = jnp.where(live, top + jnp.log(safe), LOW_FLOOR)
        inverse = 1.0 / safe
        shares = [share * inverse for share in shares]
        out = []
        for j in range(hc):
            rows = slice(j * dim, (j + 1) * dim)
            out.append(
                functools.reduce(jnp.add, [s[j : j + 1] * part(rows).astype(f32) for s, part in zip(shares, parts)])
            )
        return out, level

    def reader(ref):
        return lambda rows: ref[rows, :]

    def merge(block, extras):
        levels, weights, parts = [], [], []
        for r in range(n_row):
            v = lookup[block * n_row + r]
            levels.append(m_slot[v])
            weights.append(s_slot[v])
            parts.append(functools.partial(lambda v, rows: o_slot[v, rows, :], v))
        for ref in extras:
            levels.append(join_level(ref[cw : cw + TAIL, :], hc))
            weights.append(None)
            parts.append(reader(ref))
        return combine(levels, weights, parts)

    def put(ref, out, level):
        for j in range(hc):
            ref[j * dim : (j + 1) * dim, :] = out[j].astype(bf16)
        ref[cw : cw + TAIL, :] = split_level(level)

    now, later, incoming = route_tables(n_chip)
    now_at = padded(now, lambda z: z)
    later_at = padded(later, lambda z: z) if any(later) else []
    from_at = padded(incoming, lambda z: z)

    def sib_copy(c, z, mine):
        return remote(sib_out.at[c, z], sib_in.at[c, z], sib_send.at[c, z], sib_recv.at[c, z], sibling)

    def far_order():
        return [pick(chip, [sorted(range(n_chip), key=lambda d: -abs(d - z))[j] for z in range(n_chip)]) for j in range(n_chip)]

    order = far_order()

    def to_sibling(c):
        for z in order:
            put(sib_out.at[c, z], *merge(z * CORES + (1 - core), []))
            sib_copy(c, z, True).start()

    def direct(c, z):
        return remote(mix_out.at[c, z], got_in.at[c, chip], mix_send.at[c, z], got_recv.at[c, chip], chip_at(z))

    def got_from(c, s):
        return remote(mix_out.at[c, s], got_in.at[c, s], mix_send.at[c, s], got_recv.at[c, s], chip_at(s))

    def to_proxy(c, z):
        where = pick(chip, [1 if at == 0 else n_chip - 2 for at in range(n_chip)])
        return remote(mix_out.at[c, z], via_in.at[c, z], mix_send.at[c, z], via_recv.at[c, z], chip_at(where))

    def flags(rows):
        return [[1 if j < len(row) else 0 for row in rows] for j in range(max(map(len, rows)))]

    now_flags, later_flags, from_flags = flags(now), flags(later), flags(incoming)

    def guard(values, run):
        if all(values):
            run()
        elif any(values):
            pl.when(pick(chip, values) == 1)(run)

    def send_now(c):
        for j, dests in enumerate(now_at):
            z = pick(chip, dests)
            passes = [int(f and proxied(at, d, n_chip)) for at, (f, d) in enumerate(zip(now_flags[j], dests))]
            straight = [int(f and not proxied(at, d, n_chip)) for at, (f, d) in enumerate(zip(now_flags[j], dests))]

            def run(z=z, passes=passes, straight=straight):
                sib_copy(c, z, False).wait_recv()
                put(mix_out.at[c, z], *merge(z * CORES + core, [sib_in.at[c, z]]))
                guard(passes, lambda: to_proxy(c, z).start())
                guard(straight, lambda: direct(c, z).start())

            guard(now_flags[j], run)
        sib_copy(c, chip, False).wait_recv()
        out, level = merge(chip * CORES + core, [sib_in.at[c, chip]])
        for j in range(hc):
            own_o[c, j * dim : (j + 1) * dim, :] = out[j]
        own_l[c] = level

    def hold(c):
        for j, dests in enumerate(later_at):
            z = pick(chip, dests)

            def run(z=z):
                sib_copy(c, z, False).wait_recv()
                put(mix_out.at[c, z], *merge(z * CORES + core, [sib_in.at[c, z]]))

            guard(later_flags[j], run)

    def send_later(c):
        for j, dests in enumerate(later_at):
            z = pick(chip, dests)

            def run(z=z):
                to_proxy(c, z).wait_recv()
                refs = [mix_out.at[c, z], via_in.at[c, z]]
                levels = [join_level(ref[cw : cw + TAIL, :], hc) for ref in refs]
                put(mix_out.at[c, z], *combine(levels, [None] * 2, [reader(ref) for ref in refs]))
                direct(c, z).start()

            guard(later_flags[j], run)

    for j, origins in enumerate(from_at):
        if not all(from_flags[j]):
            s = pick(chip, origins)

            def blank(s=s):
                for c in range(chunks):
                    got_in[c, s, :cw, :] = jnp.zeros((cw, tile), bf16)
                    got_in[c, s, cw:, :] = split_level(jnp.full((hc, tile), LOW_FLOOR, f32))

            guard([1 - f for f in from_flags[j]], blank)

    def finish(c):
        levels, parts = [own_l[c]], [lambda rows: own_o[c, rows, :]]
        for j, origins in enumerate(from_at):
            s = pick(chip, origins)
            guard(from_flags[j], lambda: got_from(c, s).wait_recv())
            ref = got_in.at[c, s]
            levels.append(join_level(ref[cw : cw + TAIL, :], hc))
            parts.append(reader(ref))
        out, _ = combine(levels, [None] * len(levels), parts)
        attention = jnp.concatenate([o.astype(bf16) for o in out], axis=0)
        update = lax.dot_general(
            attention, wo_buf[c * cw : (c + 1) * cw, :], (((0,), (0,)), ((), ())), preferred_element_type=f32
        )
        if c == 0:
            out_ref[...] = update
        else:
            out_ref[...] += update

    wo_load.wait()
    for c in range(chunks):
        while waves and waves[0] < c + n_chip - 1:
            next_wave()
        for z in range(n_chip):
            pair_copy(c, z, False).wait_recv()
        attend(c)
        next_wave()
        to_sibling(c)
        send_now(c)
        hold(c)
        if c:
            send_later(c - 1)
    send_later(chunks - 1)
    for c in range(chunks):
        finish(c)

    for k in range(n_row - 1):
        e_copy(k).wait_send()
    for k in direct_rows:
        x_copy(k).wait_send()
    if relayed:
        for side in range(2):
            relay_copy(side).wait_send()
    for c in range(chunks):
        for way in (1, -1):
            for step in range(n_chip - 1):
                pl.when(inside(chip + way) & inside(chip - way * step))(lambda: line_copy(c, step, way).wait_send())
        for z in range(n_chip):
            pair_copy(c, z, True).wait_send()
            sib_copy(c, z, True).wait_send()
        for k in range(n_chip - 1):
            direct(c, target_of(chip, k + 1, n_chip)).wait_send()


def local(
    n_row,
    n_col,
    node_features,
    norm_gain,
    w_query,
    w_keyvalue,
    w_out,
    bias_table,
    edge_slope,
    pair_blocks,
    bucket_ids,
    edge_weight,
):
    tile, width = node_features.shape
    heads = edge_slope.shape[0]
    dim = width // heads
    n_chip = n_col // CORES
    slot_cap = edge_weight.shape[3]
    slots = n_row * slot_cap
    hc = CHUNK_HEADS
    cw = hc * dim
    chunks = heads // hc
    bf16, f32 = jnp.bfloat16, jnp.float32
    vmem = pl.BlockSpec(memory_space=pltpu.VMEM)
    smem = pl.BlockSpec(memory_space=pltpu.SMEM)
    hbm = pl.BlockSpec(memory_space=pltpu.HBM)
    early = 4 * slots * heads * tile * tile <= EARLY_BYTES
    message = (chunks, n_chip, cw + TAIL, tile)
    dma = pltpu.SemaphoreType.DMA
    scratch = [pltpu.VMEM((n_col, tile, cw), bf16)] * chunks + [
        pltpu.VMEM((tile, width), bf16),
        pltpu.VMEM((tile, width), bf16),
        pltpu.VMEM((n_row - 1, tile, width), bf16),
        pltpu.VMEM(w_query.shape, bf16),
        pltpu.VMEM(w_keyvalue.shape, bf16),
        pltpu.VMEM(w_out.shape, bf16),
        pltpu.VMEM((n_row, tile, width), bf16),
        pltpu.VMEM((n_row, width, tile), bf16),
        pltpu.VMEM((slots, tile, tile), jnp.int32),
        pltpu.VMEM((n_row,) + edge_weight.shape[3:], bf16),
        pltpu.VMEM((slots, heads if early else hc, tile, tile), f32),
        pltpu.VMEM((heads, tile), f32),
        pltpu.VMEM((slot_cap * max(2, hc), tile, tile), f32),
        pltpu.VMEM((slots + 1, cw, tile), f32),
        pltpu.VMEM((slots + 1, hc, tile), f32),
        pltpu.VMEM((slots + 1, hc, tile), f32),
        pltpu.SMEM((slots,), jnp.int32),
        pltpu.SMEM((n_col * n_row,), jnp.int32),
        pltpu.VMEM(message, bf16),
        pltpu.VMEM(message, bf16),
        pltpu.VMEM(message, bf16),
        pltpu.VMEM(message, bf16),
        pltpu.VMEM(message, bf16),
        pltpu.VMEM((chunks, cw, tile), f32),
        pltpu.VMEM((chunks, hc, tile), f32),
        dma((6,)),
        dma((2, n_row + 1)),
        dma((2, n_row - 1)),
        dma((chunks, n_chip - 1, 2)),
        dma((chunks, n_chip)),
        dma((chunks, n_chip)),
        dma((chunks, n_chip)),
        dma((chunks, n_chip)),
        dma((chunks, n_chip)),
        dma((chunks, n_chip)),
        dma((chunks, n_chip)),
        dma((chunks, n_chip)),
    ]
    update = pl.pallas_call(
        functools.partial(layer, n_row, n_chip, early, dim ** (-0.5)),
        out_shape=jax.ShapeDtypeStruct((tile, width), f32),
        in_specs=[smem, smem, hbm, vmem, hbm, hbm, hbm, vmem, hbm, hbm],
        out_specs=vmem,
        scratch_shapes=scratch,
        compiler_params=pltpu.CompilerParams(collective_id=0, has_side_effects=True, vmem_limit_bytes=VMEM_BYTES - SPARE),
        name="layer",
    )(
        pair_blocks.reshape(2, slots),
        edge_slope,
        node_features,
        norm_gain[None],
        w_query,
        w_keyvalue,
        w_out,
        bias_table.T,
        bucket_ids.reshape(slots, tile, tile),
        edge_weight[0, 0],
    )
    return (node_features.astype(f32) + update).astype(bf16)


def solution(mesh):
    return jax.shard_map(
        functools.partial(local, mesh.shape["row"], mesh.shape["col"]),
        mesh=mesh,
        in_specs=(
            P(("row", "col"), None),
            P(),
            P(),
            P(),
            P(),
            P(),
            P(),
            P("row", "col", None, None),
            P("row", "col", None, None, None),
            P("row", "col", None, None, None, None),
        ),
        out_specs=P(("row", "col"), None),
        check_vma=False,
    )
```
